512 devices in a mesh: replica: 4 (over y_hi), fsdp: 16 (over z, core), tensor: 8 (over y_lo, x).
Axes of the slice: x: 4, y: 8 (y_hi: 4, y_lo: 2; y = y_hi * 2 + y_lo), z: 8, core: 2. Of those that a mesh axis runs over, the one named last changes fastest.
Arguments:
- cotangent: bfloat16 [16384, 4096], P(('replica', 'fsdp'), 'tensor'), may hold values from -6 to 6
- gate_pre: bfloat16 [16384, 14336], P(('replica', 'fsdp'), 'tensor'), may hold values from -6 to 6
- up_pre: bfloat16 [16384, 14336], P(('replica', 'fsdp'), 'tensor'), may hold values from -6 to 6
- down_weight: bfloat16 [14336, 4096], P('tensor', 'fsdp'), may hold values from -0.09375 to 0.09375
- projector: bfloat16 [4096, 512], P('tensor', 'fsdp'), may hold values from -0.09375 to 0.09375
Outputs:
- grad_gate: bfloat16 [16384, 14336], P(('replica', 'fsdp'), 'tensor')
- grad_up: bfloat16 [16384, 14336], P(('replica', 'fsdp'), 'tensor')
- projected_grad: float32 [512, 14336], P('fsdp', 'tensor')
The draws below stay inside these ranges and needn't reach their ends.
All inputs are finite; a program needn't handle non-finite values.
Results may differ from the reference program's by a relative error of at most 0.0049.
Values may be sent and summed in bfloat16 or wider, within the bound.
A program may use at most 64 MiB of HBM per device.

```python
import math
import jax
import jax.numpy as jnp
from jax import lax

D = 4096
FF = 14336
RANK = 512
TOKENS = 16384


def level_of(rng, dims, shards, low, largest):
    factor_of, own = 1.0, jax.random.fold_in(rng, 6)
    for axis_at, parts in shards:
        steps = jnp.exp(jax.random.uniform(jax.random.fold_in(own, axis_at), (parts,), jnp.float32, low / len(shards), largest / len(shards)))
        factor_of = factor_of * jnp.repeat(steps, dims[axis_at] // parts).reshape([-1 if axis == axis_at else 1 for axis in range(len(dims))])
    return factor_of


def normal_values(own_key, shape, scale, reach, pieces=(), kind=jnp.bfloat16):
    drawn = scale * jax.random.normal(own_key, shape, jnp.float32)
    if pieces:
        drawn = drawn * level_of(own_key, shape, pieces, -0.22, 0.18)
    return jnp.clip(drawn, -reach, reach).astype(kind)


def setup_inputs(seed: int = 0) -> dict:
    arg_keys = jax.random.split(jax.random.key(seed), 6)
    return {
        "cotangent": normal_values(arg_keys[0], (TOKENS, D), 1.0, 6.0, ((0, 64), (1, 8))),
        "gate_pre": normal_values(arg_keys[1], (TOKENS, FF), 1.0, 6.0, ((0, 64), (1, 8))),
        "up_pre": normal_values(arg_keys[2], (TOKENS, FF), 1.0, 6.0, ((0, 64), (1, 8))),
        "down_weight": normal_values(arg_keys[3], (FF, D), D ** -0.5, 0.09375, ((0, 8), (1, 16))),
        "projector": normal_values(arg_keys[4], (D, RANK), D ** -0.5, 0.09375, ((0, 8), (1, 16))),
    }


def reference(cotangent, gate_pre, up_pre, down_weight, projector):
    block_rows = math.gcd(TOKENS, 1024)
    nblocks = TOKENS // block_rows
    cot_blocks = cotangent.reshape(nblocks, block_rows, D)
    gate_blocks = gate_pre.reshape(nblocks, block_rows, FF)
    up_blocks = up_pre.reshape(nblocks, block_rows, FF)
    down_trans = down_weight.T

    def one_block(running, inputs_block):
        cot_rows, gate_rows, up_rows = inputs_block
        hidden_grad = jnp.dot(cot_rows, down_trans, preferred_element_type=jnp.float32)
        gate_float = gate_rows.astype(jnp.float32)
        up_float = up_rows.astype(jnp.float32)
        sigma = jax.nn.sigmoid(gate_float)
        activated = gate_float * sigma
        hidden = (activated * up_float).astype(jnp.bfloat16)
        grad_up = (hidden_grad * activated).astype(jnp.bfloat16)
        grad_gate = (hidden_grad * up_float * sigma * (1.0 + gate_float * (1.0 - sigma))).astype(jnp.bfloat16)
        low_rank = jnp.dot(cot_rows, projector, preferred_element_type=jnp.float32).astype(jnp.bfloat16)
        term_block = jnp.dot(low_rank.T, hidden, preferred_element_type=jnp.float32)
        return (running + term_block, (grad_gate, grad_up))
    start = jnp.zeros((RANK, FF), jnp.float32)
    total, outputs = lax.scan(one_block, start, (cot_blocks, gate_blocks, up_blocks))
    grad_gate = outputs[0].reshape(TOKENS, FF)
    grad_up = outputs[1].reshape(TOKENS, FF)
    projected_grad = total * (1.0 / math.sqrt(TOKENS))
    return (grad_gate, grad_up, projected_grad)
```

```python
import functools
import math

import jax
import jax.numpy as jnp
from jax import lax
from jax.experimental import pallas as pl
from jax.experimental.pallas import tpu as pltpu
from jax.sharding import PartitionSpec as P

F32 = jnp.float32
BF16 = jnp.bfloat16
NZ = 8
NX = 4
NT = 8
NR = 4
LAG = 2
SUBS = ((0, 512), (512, 384), (896, 512), (1408, 384))
PLUS = tuple((d, s) for d in (1, 2, 3) for s in range(4)) + ((4, 0), (4, 1))
MINUS = tuple((d, s) for d in (1, 2, 3) for s in range(4)) + ((4, 2), (4, 3))
NM = len(PLUS)
NTILE = 256


def nt_dot(a, b):
    return lax.dot_general(a, b, (((1,), (1,)), ((), ())), preferred_element_type=F32)


def kernel(
    scale, cot_hbm, gate_hbm, up_hbm, w_hbm, pt_hbm, gg_hbm, gu_hbm, pg_hbm,
    wbuf, cotbuf, pbuf, gate, up, act, gfac, hidden, acc,
    lr_part, lr_recv, low_rank, pg, pg_half, pg_sib, ring_send, ring_recv, rep, pg_out,
    local_sem, out_sem, wz_s, wz_r, ws_s, ws_r, p_s, p_r, ps_s, ps_r,
    c_s, c_r, rs_s, rs_r, ag_s, ag_r, x_s, x_r, z_s, z_r, r_s, r_r,
):
    r = lax.axis_index("replica")
    f = lax.axis_index("fsdp")
    t = lax.axis_index("tensor")
    z, c = f // 2, f % 2
    yl, x = t // NX, t % NX

    def zdev(k):
        return {"fsdp": lax.rem(z + k + NZ, NZ) * 2 + c}

    def xdev(k):
        return {"tensor": yl * NX + lax.rem(x + k + NX, NX)}

    sibling = {"fsdp": z * 2 + 1 - c}
    pair = {"tensor": (1 - yl) * NX + x}

    def peer(k):
        return (yl + k // NX) % 2 * NX + (x + k % NX) % NX

    def remote(src, dst, send, recv, device):
        return pltpu.make_async_remote_copy(
            src_ref=src, dst_ref=dst, send_sem=send, recv_sem=recv,
            device_id=device, device_id_type=pl.DeviceIdType.MESH,
        )

    sent = []

    def start(copy):
        copy.start()
        sent.append(copy)

    lanes = pl.ds(pl.multiple_of(c * 256, 256), 256)
    prow = pl.ds(pl.multiple_of(f * 32, 32), 32)
    loads = [
        pltpu.make_async_copy(pt_hbm, pbuf.at[prow, :], local_sem.at[0]),
        pltpu.make_async_copy(w_hbm, wbuf.at[z, :, lanes], local_sem.at[1]),
        pltpu.make_async_copy(cot_hbm, cotbuf.at[t], local_sem.at[2]),
        pltpu.make_async_copy(gate_hbm, gate, local_sem.at[3]),
        pltpu.make_async_copy(up_hbm, up, local_sem.at[4]),
    ]
    for load in loads:
        load.start()

    barrier = pltpu.get_barrier_semaphore()
    greet = [zdev(k) for k in range(1, NZ)] + [sibling]
    greet += [{"tensor": peer(k)} for k in range(1, NT)]
    greet += [{"replica": lax.rem(r + k, NR)} for k in range(1, NR)]
    for device in greet:
        pl.semaphore_signal(
            barrier, inc=1, device_id=device, device_id_type=pl.DeviceIdType.MESH
        )
    pl.semaphore_wait(barrier, len(greet))

    def p_row(zz, cc):
        return pl.ds(pl.multiple_of((zz * 2 + cc) * 32, 32), 32)

    loads[0].wait()
    for k in (1, 7, 2, 6, 3, 5, 4):
        mine = pbuf.at[prow, :]
        start(remote(mine, mine, p_s.at[k - 1], p_r.at[k - 1], zdev(k)))
    start(remote(pbuf.at[prow, :], pbuf.at[prow, :], ps_s.at[0], ps_r.at[0], sibling))

    def w_piece(zz, s, cc):
        at, size = SUBS[s]
        return wbuf.at[
            lax.rem(zz + NZ, NZ), pl.ds(at, size), pl.ds(pl.multiple_of(cc * 256, 256), 256)
        ]

    def w_send(m):
        for sign, messages in ((1, PLUS), (-1, MINUS)):
            d, s = messages[m]
            ref = w_piece(z - sign * (d - 1), s, c)
            way = (1 - sign) // 2
            start(remote(ref, ref, wz_s.at[way, m], wz_r.at[way, m], zdev(sign)))

    def w_event(m):
        for sign, messages in ((1, PLUS), (-1, MINUS)):
            d, s = messages[m]
            ref = w_piece(z - sign * d, s, c)
            way = (1 - sign) // 2
            remote(ref, ref, wz_s.at[way, m], wz_r.at[way, m], zdev(sign)).wait_recv()
        if m + LAG < NM:
            w_send(m + LAG)
        for sign, messages in ((1, PLUS), (-1, MINUS)):
            d, s = messages[m]
            ref = w_piece(z - sign * d, s, c)
            way = (1 - sign) // 2
            start(remote(ref, ref, ws_s.at[way, m], ws_r.at[way, m], sibling))

    def sibling_wait(way, m):
        sign, messages = ((1, PLUS), (-1, MINUS))[way]
        d, s = messages[m]
        ref = w_piece(z - sign * d, s, 1 - c)
        remote(ref, ref, ws_s.at[way, m], ws_r.at[way, m], sibling).wait_recv()

    loads[1].wait()
    for m in range(LAG):
        w_send(m)
    own = wbuf.at[z, :, lanes]
    start(remote(own, own, ws_s.at[0, NM], ws_r.at[0, NM], sibling))

    def chunk(row, xx, half=None):
        at = row * NX + lax.rem(xx + NX, NX)
        if half is None:
            return cotbuf.at[at]
        return cotbuf.at[at, :, pl.ds(half * 256, 256)]

    def c_whole(row, i):
        ref = chunk(row, x)
        start(remote(ref, ref, c_s.at[i, 0], c_r.at[i, 0], xdev(1)))
        start(remote(ref, ref, c_s.at[i, 1], c_r.at[i, 1], xdev(-1)))

    def c_forward(row, i):
        for way, sign in ((0, 1), (1, -1)):
            ref = chunk(row, x - sign)
            remote(ref, ref, c_s.at[i, way], c_r.at[i, way], xdev(sign)).wait_recv()
            ref = chunk(row, x - sign, way)
            start(remote(ref, ref, c_s.at[i, 2 + way], c_r.at[i, 2 + way], xdev(sign)))

    def c_last(row, i):
        for way, sign in ((0, 1), (1, -1)):
            ref = chunk(row, x - 2 * sign, way)
            remote(ref, ref, c_s.at[i, 2 + way], c_r.at[i, 2 + way], xdev(sign)).wait_recv()

    loads[2].wait()
    mine = chunk(yl, x)
    start(remote(mine, mine, c_s.at[2, 0], c_r.at[2, 0], pair))
    c_whole(yl, 0)

    loads[3].wait()
    loads[4].wait()

    def factors(i, carry):
        rows = pl.ds(pl.multiple_of(i * 16, 16), 16)
        g = gate[rows, :].astype(F32)
        u = up[rows, :].astype(F32)
        sigma = jax.nn.sigmoid(g)
        activated = g * sigma
        act[rows, :] = activated
        gfac[rows, :] = u * sigma * (1.0 + g * (1.0 - sigma))
        hidden[rows, :] = (activated * u).astype(BF16)
        return carry

    lax.fori_loop(0, 16, factors, 0)

    ref = chunk(1 - yl, x)
    remote(ref, ref, c_s.at[2, 0], c_r.at[2, 0], pair).wait_recv()
    c_whole(1 - yl, 1)
    c_forward(yl, 0)

    for k in (1, 7, 2, 6, 3, 5, 4):
        zz = lax.rem(z - k + NZ, NZ)
        ref = pbuf.at[p_row(zz, c), :]
        remote(ref, ref, p_s.at[k - 1], p_r.at[k - 1], zdev(k)).wait_recv()
        start(remote(ref, ref, ps_s.at[k], ps_r.at[k], sibling))
    for k in (0, 1, 7, 2, 6, 3, 5, 4):
        ref = pbuf.at[p_row(lax.rem(z - k + NZ, NZ), 1 - c), :]
        remote(ref, ref, ps_s.at[k], ps_r.at[k], sibling).wait_recv()
    lr_part[...] = nt_dot(pbuf[...], cotbuf[t]).reshape(NT, 64, 256)

    w_event(0)
    for k in range(1, NT):
        to = peer(k)
        start(remote(
            lr_part.at[to], lr_recv.at[k - 1], rs_s.at[k - 1], rs_r.at[k - 1], {"tensor": to}
        ))
    c_forward(1 - yl, 1)
    w_event(1)

    total = lr_part[t]
    for k in range(1, NT):
        remote(
            lr_part.at[t], lr_recv.at[k - 1], rs_s.at[k - 1], rs_r.at[k - 1], pair
        ).wait_recv()
        total = total + lr_recv[k - 1]
    low_rank[t] = total.astype(BF16)
    w_event(2)
    for k in range(1, NT):
        ref = low_rank.at[t]
        start(remote(ref, ref, ag_s.at[k - 1], ag_r.at[k - 1], {"tensor": peer(k)}))

    def compute(zz, first=False):
        zz = lax.rem(zz + NZ, NZ)

        def tile(n, carry):
            at = pl.ds(pl.multiple_of(n * NTILE, NTILE), NTILE)
            part = nt_dot(cotbuf[zz], wbuf[zz, at, :])
            acc[:, at] = part if first else acc[:, at] + part
            return carry

        lax.fori_loop(0, 1792 // NTILE, tile, 0)

    c_last(yl, 0)
    c_last(1 - yl, 1)
    ref = wbuf.at[z, :, pl.ds(pl.multiple_of((1 - c) * 256, 256), 256)]
    remote(ref, ref, ws_s.at[0, NM], ws_r.at[0, NM], sibling).wait_recv()
    compute(z, first=True)
    w_event(3)

    for k in range(1, NT):
        back = (yl + k // NX) % 2 * NX + (x - k % NX + NX) % NX
        ref = low_rank.at[back]
        remote(ref, ref, ag_s.at[k - 1], ag_r.at[k - 1], {"tensor": back}).wait_recv()
    lr_all = low_rank[...].reshape(512, 256)

    def grad_tile(n, carry):
        at = pl.ds(pl.multiple_of(n * NTILE, NTILE), NTILE)
        part = jnp.dot(lr_all, hidden[:, at], preferred_element_type=F32)
        part = part.reshape(NZ, 2, 32, NTILE)
        pg[:, :, :, at] = part
        pg_half[:, :, :, at] = part.astype(BF16)
        return carry

    lax.fori_loop(0, 1792 // NTILE, grad_tile, 0)
    w_event(4)
    start(remote(pg_half.at[:, 1 - c], pg_sib, x_s.at[0], x_r.at[0], sibling))
    w_event(5)
    remote(pg_half.at[:, c], pg_sib, x_s.at[0], x_r.at[0], sibling).wait_recv()

    def chip_sum(zz):
        zz = lax.rem(zz + NZ, NZ)
        return pg[zz, c] + pg_sib[zz].astype(F32)

    def ring_wait(way, step):
        sign = 1 - 2 * way
        i = way * 4 + step
        remote(ring_send.at[i], ring_recv.at[i], z_s.at[i], z_r.at[i], zdev(sign)).wait_recv()

    def ring_value(way, step):
        sign = 1 - 2 * way
        reach = 4 - way
        value = chip_sum(z + sign * (reach - step))
        if step > 0:
            ring_wait(way, step - 1)
            value = value + ring_recv[way * 4 + step - 1].astype(F32)
        return value

    def ring_step(step):
        for way in (0, 1):
            if step < 4 - way:
                i = way * 4 + step
                ring_send[i] = ring_value(way, step).astype(BF16)
        for way in (0, 1):
            if step < 4 - way:
                i = way * 4 + step
                start(remote(
                    ring_send.at[i], ring_recv.at[i], z_s.at[i], z_r.at[i], zdev(1 - 2 * way)
                ))

    ring_step(0)

    def shard_compute(d):
        for way in (0, 1):
            for m, (dd, _) in enumerate((PLUS, MINUS)[way]):
                if dd == d:
                    sibling_wait(way, m)
        compute(z - d)
        if d < 4:
            compute(z + d)

    shard_compute(1)
    w_event(6)
    w_event(7)
    ring_step(1)
    shard_compute(2)
    w_event(8)
    w_event(9)
    ring_step(2)
    w_event(10)
    w_event(11)
    ring_step(3)
    shard_compute(3)
    w_event(12)
    ring_wait(1, 2)
    value = chip_sum(z) + ring_recv[6].astype(F32)
    ring_wait(0, 3)
    value = value + ring_recv[3].astype(F32)
    rep[r] = value.astype(BF16)
    w_event(13)
    for k in range(1, NR):
        ref = rep.at[r]
        start(remote(
            ref, ref, r_s.at[k - 1], r_r.at[k - 1], {"replica": lax.rem(r + k, NR)}
        ))
    shard_compute(4)

    outs = []
    for b in range(4):

        def finish(i, carry, b=b):
            rows = pl.ds(pl.multiple_of(b * 64 + i * 16, 16), 16)
            a = acc[rows, :]
            gate[rows, :] = (a * gfac[rows, :]).astype(BF16)
            up[rows, :] = (a * act[rows, :]).astype(BF16)
            return carry

        lax.fori_loop(0, 4, finish, 0)
        rows = pl.ds(b * 64, 64)
        outs.append(pltpu.make_async_copy(gate.at[rows], gg_hbm.at[rows], out_sem.at[2 * b]))
        outs.append(pltpu.make_async_copy(up.at[rows], gu_hbm.at[rows], out_sem.at[2 * b + 1]))
        outs[-2].start()
        outs[-1].start()

    for k in range(1, NR):
        back = lax.rem(r - k + NR, NR)
        ref = rep.at[back]
        remote(ref, ref, r_s.at[k - 1], r_r.at[k - 1], {"replica": back}).wait_recv()
    total = rep[0].astype(F32)
    for k in range(1, NR):
        total = total + rep[k].astype(F32)
    pg_out[...] = total * scale
    last = pltpu.make_async_copy(pg_out, pg_hbm, out_sem.at[8])
    last.start()
    for copy in sent:
        copy.wait_send()
    for copy in outs:
        copy.wait()
    last.wait()


def local(cotangent, gate_pre, up_pre, down_weight, projector):
    rows, width = cotangent.shape
    ff = gate_pre.shape[1]
    tokens = rows * lax.axis_size("replica") * lax.axis_size("fsdp")
    scale = 1.0 / math.sqrt(tokens)
    dma = pltpu.SemaphoreType.DMA
    hbm = pl.BlockSpec(memory_space=pl.ANY)
    return pl.pallas_call(
        functools.partial(kernel, scale),
        out_shape=(
            jax.ShapeDtypeStruct((rows, ff), BF16),
            jax.ShapeDtypeStruct((rows, ff), BF16),
            jax.ShapeDtypeStruct((32, ff), F32),
        ),
        in_specs=[hbm] * 5,
        out_specs=(hbm,) * 3,
        scratch_shapes=[
            pltpu.VMEM((NZ, ff, 512), BF16),
            pltpu.VMEM((NT, rows, width), BF16),
            pltpu.VMEM((512, width), BF16),
            pltpu.VMEM((rows, ff), BF16),
            pltpu.VMEM((rows, ff), BF16),
            pltpu.VMEM((rows, ff), F32),
            pltpu.VMEM((rows, ff), F32),
            pltpu.VMEM((rows, ff), BF16),
            pltpu.VMEM((rows, ff), F32),
            pltpu.VMEM((NT, 64, rows), F32),
            pltpu.VMEM((NT - 1, 64, rows), F32),
            pltpu.VMEM((NT, 64, rows), BF16),
            pltpu.VMEM((NZ, 2, 32, ff), F32),
            pltpu.VMEM((NZ, 2, 32, ff), BF16),
            pltpu.VMEM((NZ, 32, ff), BF16),
            pltpu.VMEM((7, 32, ff), BF16),
            pltpu.VMEM((7, 32, ff), BF16),
            pltpu.VMEM((NR, 32, ff), BF16),
            pltpu.VMEM((32, ff), F32),
            dma((5,)), dma((9,)),
            dma((2, NM)), dma((2, NM)),
            dma((2, NM + 1)), dma((2, NM + 1)),
            dma((7,)), dma((7,)), dma((8,)), dma((8,)),
            dma((3, 4)), dma((3, 4)),
            dma((7,)), dma((7,)), dma((7,)), dma((7,)),
            dma((1,)), dma((1,)), dma((7,)), dma((7,)), dma((3,)), dma((3,)),
        ],
        compiler_params=pltpu.CompilerParams(
            collective_id=0, has_side_effects=True, vmem_limit_bytes=64000 * 1024
        ),
        name="mlp_backward",
    )(cotangent, gate_pre, up_pre, down_weight, projector.T)


def solution(mesh):
    placed = (
        P(("replica", "fsdp"), "tensor"),
        P(("replica", "fsdp"), "tensor"),
        P(("replica", "fsdp"), "tensor"),
        P("tensor", "fsdp"),
        P("tensor", "fsdp"),
    )
    return jax.shard_map(
        local,
        mesh=mesh,
        in_specs=placed,
        out_specs=(
            P(("replica", "fsdp"), "tensor"),
            P(("replica", "fsdp"), "tensor"),
            P("fsdp", "tensor"),
        ),
        check_vma=False,
    )
```

```python
import functools
import math

import jax
import jax.numpy as jnp
from jax import lax
from jax.experimental import pallas as pl
from jax.experimental.pallas import tpu as pltpu
from jax.sharding import PartitionSpec as P

F32 = jnp.float32
BF16 = jnp.bfloat16
NZ = 8
NX = 4
NT = 8
NR = 4
LAG = 2
HALF = 896
PHASES = ((0, 512), (512, 384))
PLUS, MINUS = [], []
for _phase in range(len(PHASES)):
    for _d in (1, 2, 3):
        PLUS += [(_d, _phase, 0), (_d, _phase, 1)]
        MINUS += [(_d, _phase, 1), (_d, _phase, 0)]
    PLUS.append((4, _phase, 0))
    MINUS.append((4, _phase, 1))
NM = len(PLUS)
NTILE = 256


def nt_dot(a, b):
    return lax.dot_general(a, b, (((1,), (1,)), ((), ())), preferred_element_type=F32)


def kernel(
    scale, cot_hbm, gate_hbm, up_hbm, w_hbm, pt_hbm, gg_hbm, gu_hbm, pg_hbm,
    wbuf, cotbuf, cot_own, pbuf, gate, up, act, gfac, hidden, acc,
    hx_send, hx_recv, lr_part, lr_recv, low_rank, pg, pg_half, pg_sib, ring_send, ring_recv, rep, pg_out,
    local_sem, out_sem, wz_s, wz_r, ws_s, ws_r, p_s, p_r, ps_s, ps_r,
    c_s, c_r, rs_s, rs_r, ag_s, ag_r, x_s, x_r, z_s, z_r, r_s, r_r,
    cr_s, cr_r, h_s, h_r,
):
    r = lax.axis_index("replica")
    f = lax.axis_index("fsdp")
    t = lax.axis_index("tensor")
    z, c = f // 2, f % 2
    par = r % 2
    yl, x = t // NX, t % NX

    def zdev(k):
        return {"fsdp": lax.rem(z + k + NZ, NZ) * 2 + c}

    def xdev(k):
        return {"tensor": yl * NX + lax.rem(x + k + NX, NX)}

    def near(k):
        return {"replica": lax.rem(r + k + NR, NR)}

    sibling = {"fsdp": z * 2 + 1 - c}
    pair = {"tensor": (1 - yl) * NX + x}

    def peer(k):
        return (yl + k // NX) % 2 * NX + (x + k % NX) % NX

    def remote(src, dst, send, recv, device):
        return pltpu.make_async_remote_copy(
            src_ref=src, dst_ref=dst, send_sem=send, recv_sem=recv,
            device_id=device, device_id_type=pl.DeviceIdType.MESH,
        )

    sent = []

    def start(copy):
        copy.start()
        sent.append(copy)

    def lane(at):
        return pl.ds(pl.multiple_of(at, 128), 128)

    lanes = lane(c * 128)
    prow = pl.ds(pl.multiple_of(f * 32, 32), 32)
    loads = [
        pltpu.make_async_copy(pt_hbm, pbuf.at[prow, :], local_sem.at[0]),
        pltpu.make_async_copy(
            w_hbm.at[:, lane(par * 128)], wbuf.at[z, :, lanes], local_sem.at[1]
        ),
        pltpu.make_async_copy(cot_hbm, cot_own, local_sem.at[2]),
        pltpu.make_async_copy(gate_hbm, gate, local_sem.at[3]),
        pltpu.make_async_copy(up_hbm, up, local_sem.at[4]),
    ]
    loads += [
        pltpu.make_async_copy(
            cot_hbm.at[:, lane(q * 256 + par * 128)],
            cotbuf.at[t, pl.ds(256, 256), pl.ds(q * 128, 128)],
            local_sem.at[5 + q],
        )
        for q in (0, 1)
    ]
    for load in loads:
        load.start()

    barrier = pltpu.get_barrier_semaphore()
    greet = [zdev(k) for k in range(1, NZ)] + [sibling]
    greet += [{"tensor": peer(k)} for k in range(1, NT)]
    greet += [{"replica": lax.rem(r + k, NR)} for k in range(1, NR)]
    for device in greet:
        pl.semaphore_signal(
            barrier, inc=1, device_id=device, device_id_type=pl.DeviceIdType.MESH
        )
    pl.semaphore_wait(barrier, len(greet))

    def p_row(zz, cc):
        return pl.ds(pl.multiple_of((zz * 2 + cc) * 32, 32), 32)

    loads[0].wait()
    for k in (1, 7, 2, 6, 3, 5, 4):
        mine = pbuf.at[prow, :]
        start(remote(mine, mine, p_s.at[k - 1], p_r.at[k - 1], zdev(k)))
    start(remote(pbuf.at[prow, :], pbuf.at[prow, :], ps_s.at[0], ps_r.at[0], sibling))

    def w_piece(zz, phase, h, cc):
        at, size = PHASES[phase]
        return wbuf.at[lax.rem(zz + NZ, NZ), pl.ds(h * HALF + at, size), lane(cc * 128)]

    def w_send(m):
        for way, sign, messages in ((0, 1, PLUS), (1, -1, MINUS)):
            d, phase, h = messages[m]
            ref = w_piece(z - sign * (d - 1), phase, h, c)
            start(remote(ref, ref, wz_s.at[way, m], wz_r.at[way, m], zdev(sign)))

    def w_event(m):
        for way, sign, messages in ((0, 1, PLUS), (1, -1, MINUS)):
            d, phase, h = messages[m]
            ref = w_piece(z - sign * d, phase, h, c)
            remote(ref, ref, wz_s.at[way, m], wz_r.at[way, m], zdev(sign)).wait_recv()
        if m + LAG < NM:
            w_send(m + LAG)
        for way, sign, messages in ((0, 1, PLUS), (1, -1, MINUS)):
            d, phase, h = messages[m]
            ref = w_piece(z - sign * d, phase, h, c)
            start(remote(ref, ref, ws_s.at[way, m], ws_r.at[way, m], sibling))

    def sibling_wait(way, m):
        sign, messages = ((1, PLUS), (-1, MINUS))[way]
        d, phase, h = messages[m]
        ref = w_piece(z - sign * d, phase, h, 1 - c)
        remote(ref, ref, ws_s.at[way, m], ws_r.at[way, m], sibling).wait_recv()

    loads[1].wait()
    for m in range(LAG):
        w_send(m)
    own = wbuf.at[z, :, lanes]
    start(remote(own, own, ws_s.at[0, NM], ws_r.at[0, NM], sibling))

    def chunk(row, xx, j, half=None):
        at = row * NX + lax.rem(xx + NX, NX)
        if half is None:
            return cotbuf.at[at, pl.ds(j * 256, 256), :]
        return cotbuf.at[at, pl.ds(j * 256 + half * 128, 128), :]

    def c_whole(row, j, i):
        ref = chunk(row, x, j)
        start(remote(ref, ref, c_s.at[i, j, 0], c_r.at[i, j, 0], xdev(1)))
        start(remote(ref, ref, c_s.at[i, j, 1], c_r.at[i, j, 1], xdev(-1)))

    def c_forward(row, j, i):
        for way, sign in ((0, 1), (1, -1)):
            ref = chunk(row, x - sign, j)
            remote(ref, ref, c_s.at[i, j, way], c_r.at[i, j, way], xdev(sign)).wait_recv()
            ref = chunk(row, x - sign, j, way)
            start(remote(
                ref, ref, c_s.at[i, j, 2 + way], c_r.at[i, j, 2 + way], xdev(sign)
            ))

    def c_last(row, j, i):
        for way, sign in ((0, 1), (1, -1)):
            ref = chunk(row, x - 2 * sign, j, way)
            remote(
                ref, ref, c_s.at[i, j, 2 + way], c_r.at[i, j, 2 + way], xdev(sign)
            ).wait_recv()

    def c_pair(j):
        ref = chunk(yl, x, j)
        start(remote(ref, ref, c_s.at[2, j, 0], c_r.at[2, j, 0], pair))

    def c_pair_wait(j):
        ref = chunk(1 - yl, x, j)
        remote(ref, ref, c_s.at[2, j, 0], c_r.at[2, j, 0], pair).wait_recv()

    def c_replica(way, q):
        there = 2 - 2 * way
        return remote(
            cot_own.at[:, lane(q * 256 + (1 - par) * 128)],
            cotbuf.at[t, pl.ds(there * 256, 256), pl.ds(q * 128, 128)],
            cr_s.at[way, q], cr_r.at[way, q], near(1 - 2 * way),
        )

    loads[2].wait()
    for way in (0, 1):
        for q in (0, 1):
            start(c_replica(way, q))
    loads[5].wait()
    loads[6].wait()
    c_pair(1)
    c_whole(yl, 1, 0)

    loads[3].wait()
    loads[4].wait()

    def factors(i, carry):
        rows = pl.ds(pl.multiple_of(i * 16, 16), 16)
        g = gate[rows, :].astype(F32)
        u = up[rows, :].astype(F32)
        sigma = jax.nn.sigmoid(g)
        activated = g * sigma
        act[rows, :] = activated
        gfac[rows, :] = u * sigma * (1.0 + g * (1.0 - sigma))
        hidden[rows, :] = (activated * u).astype(BF16)
        return carry

    lax.fori_loop(0, 16, factors, 0)

    c_pair_wait(1)
    c_whole(1 - yl, 1, 1)
    c_forward(yl, 1, 0)
    for j in (0, 2):
        for q in (0, 1):
            c_replica(1 - j // 2, q).wait_recv()
        c_pair(j)
        c_whole(yl, j, 0)

    for k in (1, 7, 2, 6, 3, 5, 4):
        zz = lax.rem(z - k + NZ, NZ)
        ref = pbuf.at[p_row(zz, c), :]
        remote(ref, ref, p_s.at[k - 1], p_r.at[k - 1], zdev(k)).wait_recv()
        start(remote(ref, ref, ps_s.at[k], ps_r.at[k], sibling))
    for k in (0, 1, 7, 2, 6, 3, 5, 4):
        ref = pbuf.at[p_row(lax.rem(z - k + NZ, NZ), 1 - c), :]
        remote(ref, ref, ps_s.at[k], ps_r.at[k], sibling).wait_recv()
    lr_part[...] = nt_dot(pbuf[...], cot_own[...]).reshape(NT, 64, 256)

    w_event(0)
    for k in range(1, NT):
        to = peer(k)
        start(remote(
            lr_part.at[to], lr_recv.at[k - 1], rs_s.at[k - 1], rs_r.at[k - 1], {"tensor": to}
        ))
    w_event(1)
    c_forward(1 - yl, 1, 1)
    for j in (0, 2):
        c_pair_wait(j)
        c_whole(1 - yl, j, 1)
        c_forward(yl, j, 0)
    w_event(2)

    total = lr_part[t]
    for k in range(1, NT):
        remote(
            lr_part.at[t], lr_recv.at[k - 1], rs_s.at[k - 1], rs_r.at[k - 1], pair
        ).wait_recv()
        total = total + lr_recv[k - 1]
    low_rank[t] = total.astype(BF16)
    for k in range(1, NT):
        ref = low_rank.at[t]
        start(remote(ref, ref, ag_s.at[k - 1], ag_r.at[k - 1], {"tensor": peer(k)}))
    w_event(3)
    for j in (0, 2):
        c_forward(1 - yl, j, 1)
    w_event(4)

    def compute(phase, zz, first=False):
        zz = lax.rem(zz + NZ, NZ)
        at, size = PHASES[phase]

        def part(h, carry):
            left = cotbuf[zz, pl.ds(pl.multiple_of(h * 256, 256), 512), :]
            for n in range(0, size, NTILE):
                width = min(NTILE, size - n)
                cols = pl.ds(at + n, width)
                weight = wbuf[zz, pl.ds(pl.multiple_of(h * HALF + at + n, 128), width), :]
                value = nt_dot(left, weight)
                acc[h, :, cols] = value if first else acc[h, :, cols] + value
            return carry

        lax.fori_loop(0, 2, part, 0)

    for k in range(1, NT):
        back = (yl + k // NX) % 2 * NX + (x - k % NX + NX) % NX
        ref = low_rank.at[back]
        remote(ref, ref, ag_s.at[k - 1], ag_r.at[k - 1], {"tensor": back}).wait_recv()
    lr_all = low_rank[...].reshape(512, 256)

    def grad_tile(n, carry):
        at = pl.ds(pl.multiple_of(n * NTILE, NTILE), NTILE)
        part = jnp.dot(lr_all, hidden[:, at], preferred_element_type=F32)
        part = part.reshape(NZ, 2, 32, NTILE)
        pg[:, :, :, at] = part
        pg_half[:, :, :, at] = part.astype(BF16)
        return carry

    lax.fori_loop(0, 1792 // NTILE, grad_tile, 0)
    w_event(5)
    start(remote(pg_half.at[:, 1 - c], pg_sib, x_s.at[0], x_r.at[0], sibling))
    for j in range(3):
        c_last(yl, j, 0)
        c_last(1 - yl, j, 1)
    w_event(6)
    remote(pg_half.at[:, c], pg_sib, x_s.at[0], x_r.at[0], sibling).wait_recv()

    def chip_sum(zz):
        zz = lax.rem(zz + NZ, NZ)
        return pg[zz, c] + pg_sib[zz].astype(F32)

    def ring_wait(way, step):
        sign = 1 - 2 * way
        i = way * 4 + step
        remote(ring_send.at[i], ring_recv.at[i], z_s.at[i], z_r.at[i], zdev(sign)).wait_recv()

    def ring_value(way, step):
        sign = 1 - 2 * way
        reach = 4 - way
        value = chip_sum(z + sign * (reach - step))
        if step > 0:
            ring_wait(way, step - 1)
            value = value + ring_recv[way * 4 + step - 1].astype(F32)
        return value

    def ring_step(step):
        for way in (0, 1):
            if step < 4 - way:
                i = way * 4 + step
                ring_send[i] = ring_value(way, step).astype(BF16)
        for way in (0, 1):
            if step < 4 - way:
                i = way * 4 + step
                start(remote(
                    ring_send.at[i], ring_recv.at[i], z_s.at[i], z_r.at[i], zdev(1 - 2 * way)
                ))

    ring_step(0)

    def shard_compute(phase, d):
        if d == 0:
            compute(phase, z, first=True)
            return
        for way in (0, 1):
            for m, (dd, pp, _) in enumerate((PLUS, MINUS)[way]):
                if (dd, pp) == (d, phase):
                    sibling_wait(way, m)
        compute(phase, z - d)
        if d < 4:
            compute(phase, z + d)

    def hand_over(phase):
        at, size = PHASES[phase]
        cols = pl.ds(at, size)
        for way in (0, 1):
            for b in range(0, 256, 64):
                hx_send[way, pl.ds(b, 64), cols] = acc[
                    way, pl.ds(way * 256 + b, 64), cols
                ].astype(BF16)
        for way in (0, 1):
            start(remote(
                hx_send.at[way, :, cols], hx_recv.at[way, :, cols],
                h_s.at[way, phase], h_r.at[way, phase], near(1 - 2 * way),
            ))

    def hand_over_wait(phase):
        cols = pl.ds(*PHASES[phase])
        for way in (0, 1):
            remote(
                hx_send.at[way, :, cols], hx_recv.at[way, :, cols],
                h_s.at[way, phase], h_r.at[way, phase], near(1 - 2 * way),
            ).wait_recv()

    ref = wbuf.at[z, :, lane((1 - c) * 128)]
    remote(ref, ref, ws_s.at[0, NM], ws_r.at[0, NM], sibling).wait_recv()
    shard_compute(0, 0)
    w_event(7)
    shard_compute(0, 1)
    w_event(8)
    ring_step(1)
    shard_compute(0, 2)
    w_event(9)
    shard_compute(0, 3)
    w_event(10)
    ring_step(2)
    shard_compute(0, 4)
    hand_over(0)
    w_event(11)
    shard_compute(1, 0)
    shard_compute(1, 1)
    w_event(12)
    ring_step(3)
    shard_compute(1, 2)
    w_event(13)
    shard_compute(1, 3)
    shard_compute(1, 4)
    hand_over(1)
    ring_wait(1, 2)
    value = chip_sum(z) + ring_recv[6].astype(F32)
    ring_wait(0, 3)
    value = value + ring_recv[3].astype(F32)
    rep[r] = value.astype(BF16)
    for k in range(1, NR):
        ref = rep.at[r]
        start(remote(ref, ref, r_s.at[k - 1], r_r.at[k - 1], near(k)))
    hand_over_wait(0)
    hand_over_wait(1)

    outs = []
    for b in range(4):

        def finish(i, carry, b=b):
            rows = pl.ds(pl.multiple_of(b * 64 + i * 16, 16), 16)
            for h in (0, 1):
                cols = pl.ds(h * HALF, HALF)
                mine = pl.ds(pl.multiple_of((1 - h) * 256 + b * 64 + i * 16, 16), 16)
                a = acc[h, mine, :] + hx_recv[h, rows, :].astype(F32)
                gate[rows, cols] = (a * gfac[rows, cols]).astype(BF16)
                up[rows, cols] = (a * act[rows, cols]).astype(BF16)
            return carry

        lax.fori_loop(0, 4, finish, 0)
        rows = pl.ds(b * 64, 64)
        outs.append(pltpu.make_async_copy(gate.at[rows], gg_hbm.at[rows], out_sem.at[2 * b]))
        outs.append(pltpu.make_async_copy(up.at[rows], gu_hbm.at[rows], out_sem.at[2 * b + 1]))
        outs[-2].start()
        outs[-1].start()

    for k in range(1, NR):
        back = lax.rem(r - k + NR, NR)
        ref = rep.at[back]
        remote(ref, ref, r_s.at[k - 1], r_r.at[k - 1], {"replica": back}).wait_recv()
    total = rep[0].astype(F32)
    for k in range(1, NR):
        total = total + rep[k].astype(F32)
    pg_out[...] = total * scale
    last = pltpu.make_async_copy(pg_out, pg_hbm, out_sem.at[8])
    last.start()
    for copy in sent:
        copy.wait_send()
    for copy in outs:
        copy.wait()
    last.wait()


def local(cotangent, gate_pre, up_pre, down_weight, projector):
    rows, width = cotangent.shape
    ff = gate_pre.shape[1]
    tokens = rows * lax.axis_size("replica") * lax.axis_size("fsdp")
    scale = 1.0 / math.sqrt(tokens)
    dma = pltpu.SemaphoreType.DMA
    hbm = pl.BlockSpec(memory_space=pl.ANY)
    return pl.pallas_call(
        functools.partial(kernel, scale),
        out_shape=(
            jax.ShapeDtypeStruct((rows, ff), BF16),
            jax.ShapeDtypeStruct((rows, ff), BF16),
            jax.ShapeDtypeStruct((32, ff), F32),
        ),
        in_specs=[hbm] * 5,
        out_specs=(hbm,) * 3,
        scratch_shapes=[
            pltpu.VMEM((NZ, ff, 256), BF16),
            pltpu.VMEM((NT, 3 * rows, 256), BF16),
            pltpu.VMEM((rows, width), BF16),
            pltpu.VMEM((512, width), BF16),
            pltpu.VMEM((rows, ff), BF16),
            pltpu.VMEM((rows, ff), BF16),
            pltpu.VMEM((rows, ff), F32),
            pltpu.VMEM((rows, ff), F32),
            pltpu.VMEM((rows, ff), BF16),
            pltpu.VMEM((2, 2 * rows, HALF), F32),
            pltpu.VMEM((2, rows, HALF), BF16),
            pltpu.VMEM((2, rows, HALF), BF16),
            pltpu.VMEM((NT, 64, rows), F32),
            pltpu.VMEM((NT - 1, 64, rows), F32),
            pltpu.VMEM((NT, 64, rows), BF16),
            pltpu.VMEM((NZ, 2, 32, ff), F32),
            pltpu.VMEM((NZ, 2, 32, ff), BF16),
            pltpu.VMEM((NZ, 32, ff), BF16),
            pltpu.VMEM((7, 32, ff), BF16),
            pltpu.VMEM((7, 32, ff), BF16),
            pltpu.VMEM((NR, 32, ff), BF16),
            pltpu.VMEM((32, ff), F32),
            dma((7,)), dma((9,)),
            dma((2, NM)), dma((2, NM)),
            dma((2, NM + 1)), dma((2, NM + 1)),
            dma((7,)), dma((7,)), dma((8,)), dma((8,)),
            dma((3, 3, 4)), dma((3, 3, 4)),
            dma((7,)), dma((7,)), dma((7,)), dma((7,)),
            dma((1,)), dma((1,)), dma((7,)), dma((7,)), dma((3,)), dma((3,)),
            dma((2, 2)), dma((2, 2)), dma((2, len(PHASES))), dma((2, len(PHASES))),
        ],
        compiler_params=pltpu.CompilerParams(
            collective_id=0, has_side_effects=True, vmem_limit_bytes=64000 * 1024
        ),
        name="mlp_backward",
    )(cotangent, gate_pre, up_pre, down_weight, projector.T)


def solution(mesh):
    placed = (
        P(("replica", "fsdp"), "tensor"),
        P(("replica", "fsdp"), "tensor"),
        P(("replica", "fsdp"), "tensor"),
        P("tensor", "fsdp"),
        P("tensor", "fsdp"),
    )
    return jax.shard_map(
        local,
        mesh=mesh,
        in_specs=placed,
        out_specs=(
            P(("replica", "fsdp"), "tensor"),
            P(("replica", "fsdp"), "tensor"),
            P("fsdp", "tensor"),
        ),
        check_vma=False,
    )
```

```python
import functools
import math

import jax
import jax.numpy as jnp
from jax import lax
from jax.experimental import pallas as pl
from jax.experimental.pallas import tpu as pltpu
from jax.sharding import PartitionSpec as P

F32 = jnp.float32
BF16 = jnp.bfloat16
NZ = 8
NX = 4
NT = 8
NR = 4
FF = 1792
ROWS = 256
STREAMS = FF // ROWS
HALF = FF // 2
LAG = 3
MESSAGES = sorted(
    ((d, i) for i in range(STREAMS) for d in (1, 2, 3, 4)),
    key=lambda m: (2 * m[1] + 3 * m[0], m[1]),
)
NM = len(MESSAGES)
NEAR_FIRST = (1, 7, 2, 6, 3, 5, 4)


def nt_dot(a, b):
    return lax.dot_general(a, b, (((1,), (1,)), ((), ())), preferred_element_type=F32)


def kernel(
    cot_hbm, gate_hbm, up_hbm, w_hbm, pt_hbm, acc_hbm, hx_hbm, rep_hbm,
    wbuf, cotbuf, cot_own, pbuf, gate, up, hidden, acc, hx,
    lr_part, lr_recv, low_rank, pg, ring_send, ring_recv, rep,
    local_sem, out_sem, wz_s, wz_r, ws_s, ws_r, p_s, p_r, sib_s, sib_r,
    c_s, c_r, cr_s, cr_r, rs_s, rs_r, ag_s, ag_r, z_s, z_r, r_s, r_r, h_s, h_r,
):
    r = lax.axis_index("replica")
    f = lax.axis_index("fsdp")
    t = lax.axis_index("tensor")
    z, c = f // 2, f % 2
    yl, x = t // NX, t % NX
    par = r % 2
    mate = {"replica": lax.rem(r + 1 - 2 * ((r + c) % 2) + NR, NR)}

    def zdev(k):
        return {"fsdp": lax.rem(z + k + NZ, NZ) * 2 + c}

    def xdev(k):
        return {"tensor": yl * NX + lax.rem(x + k + NX, NX)}

    sibling = {"fsdp": z * 2 + 1 - c}
    pair = {"tensor": (1 - yl) * NX + x}

    def peer(k):
        return (yl + k // NX) % 2 * NX + (x + k % NX) % NX

    def peer_back(k):
        return (yl + k // NX) % 2 * NX + (x - k % NX + NX) % NX

    def lane(at, size=128):
        return pl.ds(pl.multiple_of(at, 128), size)

    def rows_at(at, size):
        return pl.ds(pl.multiple_of(at, 32), size)

    def remote(src, dst, send, recv, device):
        return pltpu.make_async_remote_copy(
            src_ref=src, dst_ref=dst, send_sem=send, recv_sem=recv,
            device_id=device, device_id_type=pl.DeviceIdType.MESH,
        )

    sent = []

    def start(copy):
        copy.start()
        sent.append(copy)

    own_w = wbuf.at[:, lane((z * 2 + c) * 128)]
    sib_w = wbuf.at[:, lane((z * 2 + 1 - c) * 128)]
    loads = [
        pltpu.make_async_copy(pt_hbm, pbuf.at[rows_at(z * 32, 32), :], local_sem.at[0]),
        pltpu.make_async_copy(w_hbm.at[:, lane(par * 128)], own_w, local_sem.at[1]),
        pltpu.make_async_copy(cot_hbm, cot_own.at[c], local_sem.at[2]),
        pltpu.make_async_copy(gate_hbm, gate, local_sem.at[3]),
        pltpu.make_async_copy(up_hbm, up, local_sem.at[4]),
    ]
    loads += [
        pltpu.make_async_copy(
            cot_hbm.at[:, lane(q * 256 + par * 128)],
            cotbuf.at[pl.ds(0, ROWS), lane(t * 256 + q * 128)],
            local_sem.at[5 + q],
        )
        for q in (0, 1)
    ]
    for load in loads:
        load.start()

    barrier = pltpu.get_barrier_semaphore()
    greet = [zdev(k) for k in range(1, NZ)] + [sibling]
    greet += [{"tensor": peer(k)} for k in range(1, NT)]
    greet += [{"replica": lax.rem(r + k, NR)} for k in range(1, NR)]
    for device in greet:
        pl.semaphore_signal(
            barrier, inc=1, device_id=device, device_id_type=pl.DeviceIdType.MESH
        )
    pl.semaphore_wait(barrier, len(greet))

    loads[0].wait()
    for k in NEAR_FIRST:
        mine = pbuf.at[rows_at(z * 32, 32), :]
        start(remote(mine, mine, p_s.at[k - 1], p_r.at[k - 1], zdev(k)))

    def chunk(row, xx, j, part=None):
        at = row * NX + lax.rem(xx + NX, NX)
        if part is None:
            return cotbuf.at[pl.ds(j * ROWS, ROWS), lane(at * 256, 256)]
        return cotbuf.at[pl.ds(j * ROWS + part * 128, 128), lane(at * 256, 256)]

    def c_whole(row, j, i):
        ref = chunk(row, x, j)
        for way, sign in ((0, 1), (1, -1)):
            start(remote(ref, ref, c_s.at[i, j, way], c_r.at[i, j, way], xdev(sign)))

    def c_forward(row, j, i):
        for way, sign in ((0, 1), (1, -1)):
            ref = chunk(row, x - sign, j)
            remote(ref, ref, c_s.at[i, j, way], c_r.at[i, j, way], xdev(sign)).wait_recv()
            ref = chunk(row, x - sign, j, way)
            start(remote(
                ref, ref, c_s.at[i, j, 2 + way], c_r.at[i, j, 2 + way], xdev(sign)
            ))

    def c_last(row, j, i):
        for way, sign in ((0, 1), (1, -1)):
            ref = chunk(row, x - 2 * sign, j, way)
            remote(
                ref, ref, c_s.at[i, j, 2 + way], c_r.at[i, j, 2 + way], xdev(sign)
            ).wait_recv()

    def c_pair(j):
        ref = chunk(yl, x, j)
        start(remote(ref, ref, c_s.at[2, j, 0], c_r.at[2, j, 0], pair))

    def c_pair_wait(j):
        ref = chunk(1 - yl, x, j)
        remote(ref, ref, c_s.at[2, j, 0], c_r.at[2, j, 0], pair).wait_recv()

    def c_mate(q):
        return remote(
            cot_own.at[c, :, lane(q * 256 + (1 - par) * 128)],
            cotbuf.at[pl.ds(ROWS, ROWS), lane(t * 256 + q * 128)],
            cr_s.at[q], cr_r.at[q], mate,
        )

    loads[2].wait()
    start(c_mate(0))
    start(c_mate(1))
    loads[5].wait()
    loads[6].wait()
    c_pair(0)
    c_whole(yl, 0, 0)
    start(remote(cot_own.at[c], cot_own.at[c], sib_s.at[0], sib_r.at[0], sibling))

    def w_piece(way, m, zz, cc):
        d, i = MESSAGES[m]
        at, size = (i * ROWS, ROWS) if d < 4 else (i * ROWS + way * 128, 128)
        return wbuf.at[pl.ds(at, size), lane((lax.rem(zz + NZ, NZ) * 2 + cc) * 128)]

    def needs(m):
        d, i = MESSAGES[m]
        return MESSAGES.index((d - 1, i)) if d > 1 else -1

    def w_send(m):
        d = MESSAGES[m][0]
        for way, sign in ((0, 1), (1, -1)):
            ref = w_piece(way, m, z - sign * (d - 1), c)
            start(remote(ref, ref, wz_s.at[way, m], wz_r.at[way, m], zdev(sign)))

    state = {"sent": 0, "event": 0, "ready": False, "todo": []}

    def w_push(done, lag):
        while state["sent"] < min(NM, done + 1 + lag) and needs(state["sent"]) <= done:
            w_send(state["sent"])
            state["sent"] += 1

    def w_event(lag):
        m = state["event"]
        state["event"] += 1
        d, i = MESSAGES[m]
        for way, sign in ((0, 1), (1, -1)):
            ref = w_piece(way, m, z - sign * d, c)
            remote(ref, ref, wz_s.at[way, m], wz_r.at[way, m], zdev(sign)).wait_recv()
        w_push(m, lag)
        for way, sign in ((0, 1), (1, -1)):
            ref = w_piece(way, m, z - sign * d, c)
            start(remote(ref, ref, ws_s.at[way, m], ws_r.at[way, m], sibling))
        if d == 4:
            state["todo"].append(i)

    outs = []

    def compute(i):
        for m, (d, ii) in enumerate(MESSAGES):
            if ii == i:
                for way, sign in ((0, 1), (1, -1)):
                    ref = w_piece(way, m, z - sign * d, 1 - c)
                    remote(ref, ref, ws_s.at[way, m], ws_r.at[way, m], sibling).wait_recv()
        cols = pl.ds(i * ROWS, ROWS)

        def part(j, weight):
            return nt_dot(cotbuf[pl.ds(j * ROWS, ROWS), :], wbuf[cols, :])

        hx[:, cols] = part(1, None).astype(BF16)
        acc[:, cols] = part(0, None)
        start(remote(hx.at[:, cols], hx_hbm.at[:, cols], h_s.at[i], h_r.at[i], mate))
        out = pltpu.make_async_copy(acc.at[:, cols], acc_hbm.at[:, cols], out_sem.at[i])
        out.start()
        outs.append(out)

    def pump(events, lag=LAG):
        for _ in range(events):
            if state["event"] < NM:
                w_event(lag)
            if state["ready"] and len(state["todo"]) > 1:
                compute(state["todo"].pop(0))

    loads[1].wait()
    w_push(-1, LAG)
    start(remote(own_w, own_w, sib_s.at[1], sib_r.at[1], sibling))

    loads[3].wait()
    loads[4].wait()

    def make_hidden(i, carry):
        rows = pl.ds(pl.multiple_of(i * 16, 16), 16)
        g = gate[rows, :].astype(F32)
        activated = g * jax.nn.sigmoid(g)
        hidden[c, rows, :] = (activated * up[rows, :].astype(F32)).astype(BF16)
        return carry

    lax.fori_loop(0, 16, make_hidden, 0)
    c_pair_wait(0)
    c_whole(1 - yl, 0, 1)
    c_forward(yl, 0, 0)
    start(remote(hidden.at[c], hidden.at[c], sib_s.at[2], sib_r.at[2], sibling))

    for k in NEAR_FIRST:
        ref = pbuf.at[rows_at(lax.rem(z - k + NZ, NZ) * 32, 32), :]
        remote(ref, ref, p_s.at[k - 1], p_r.at[k - 1], zdev(k)).wait_recv()
    ref = cot_own.at[1 - c]
    remote(ref, ref, sib_s.at[0], sib_r.at[0], sibling).wait_recv()
    lr_part[...] = nt_dot(pbuf[...], cot_own[...].reshape(2 * ROWS, 512)).reshape(NT, 32, 512)
    pump(1)
    for k in range(1, NT):
        to = peer(k)
        start(remote(
            lr_part.at[to], lr_recv.at[k - 1], rs_s.at[k - 1], rs_r.at[k - 1], {"tensor": to}
        ))
    c_mate(0).wait_recv()
    c_mate(1).wait_recv()
    c_pair(1)
    c_whole(yl, 1, 0)
    pump(1)
    c_forward(1 - yl, 0, 1)
    pump(2)
    total = lr_part[t]
    for k in range(1, NT):
        remote(
            lr_part.at[t], lr_recv.at[k - 1], rs_s.at[k - 1], rs_r.at[k - 1], pair
        ).wait_recv()
        total = total + lr_recv[k - 1]
    low_rank[t] = total.astype(BF16)
    pump(1)
    for k in range(1, NT):
        ref = low_rank.at[t]
        start(remote(ref, ref, ag_s.at[k - 1], ag_r.at[k - 1], {"tensor": peer(k)}))
    c_pair_wait(1)
    c_whole(1 - yl, 1, 1)
    pump(2)
    c_forward(yl, 1, 0)
    pump(2)
    c_forward(1 - yl, 1, 1)
    pump(1)

    for k in range(1, NT):
        ref = low_rank.at[peer_back(k)]
        remote(
            ref, ref, ag_s.at[k - 1], ag_r.at[k - 1], {"tensor": peer_back(k)}
        ).wait_recv()
    ref = hidden.at[1 - c]
    remote(ref, ref, sib_s.at[2], sib_r.at[2], sibling).wait_recv()

    def grad_tile(n, carry):
        at = lane(n * 256, 256)
        both = jnp.concatenate([hidden[0, :, at], hidden[1, :, at]], axis=0)
        part = jnp.dot(
            low_rank[...].reshape(256, 2 * ROWS), both, preferred_element_type=F32
        )
        pg[:, :, at] = part.reshape(NZ, 32, 256)
        return carry

    lax.fori_loop(0, FF // 256, grad_tile, 0)

    def own_part(zz, h):
        return pg[lax.rem(zz + NZ, NZ), :, pl.ds(h * HALF, HALF)]

    def ring(way, step, h):
        i = way * 4 + step
        return remote(
            ring_send.at[h, i], ring_recv.at[h, i], z_s.at[h, i], z_r.at[h, i],
            zdev(1 - 2 * way),
        )

    def ring_step(step, h):
        for way in (0, 1):
            if step < 4 - way:
                i = way * 4 + step
                value = own_part(z + (1 - 2 * way) * (4 - way - step), h)
                if step > 0:
                    ring(way, step - 1, h).wait_recv()
                    value = value + ring_recv[h, i - 1].astype(F32)
                ring_send[h, i] = value.astype(BF16)
        for way in (0, 1):
            if step < 4 - way:
                start(ring(way, step, h))

    def replica_send(h):
        ring(1, 2, h).wait_recv()
        value = own_part(z, h) + ring_recv[h, 6].astype(F32)
        ring(0, 3, h).wait_recv()
        value = value + ring_recv[h, 3].astype(F32)
        rep[h] = value.astype(BF16)
        there = rep_hbm.at[r, :, pl.ds(h * HALF, HALF)]
        for k in range(1, NR):
            start(remote(
                rep.at[h], there, r_s.at[h, k - 1], r_r.at[h, k - 1],
                {"replica": lax.rem(r + k, NR)},
            ))
        out = pltpu.make_async_copy(rep.at[h], there, out_sem.at[STREAMS + h])
        out.start()
        outs.append(out)

    ring_step(0, 0)
    ring_step(0, 1)
    pump(2)
    c_last(yl, 0, 0)
    c_last(1 - yl, 0, 1)
    c_last(yl, 1, 0)
    c_last(1 - yl, 1, 1)
    remote(sib_w, sib_w, sib_s.at[1], sib_r.at[1], sibling).wait_recv()
    state["ready"] = True
    pump(1)
    ring_step(1, 0)
    ring_step(1, 1)
    pump(3)
    ring_step(2, 0)
    ring_step(2, 1)
    pump(3)
    ring_step(3, 0)
    ring_step(3, 1)
    pump(3)
    replica_send(0)
    replica_send(1)
    pump(NM)
    for i in state["todo"]:
        compute(i)

    for i in range(STREAMS):
        cols = pl.ds(i * ROWS, ROWS)
        remote(hx.at[:, cols], hx_hbm.at[:, cols], h_s.at[i], h_r.at[i], mate).wait_recv()
    for h in (0, 1):
        for k in range(1, NR):
            back = lax.rem(r - k + NR, NR)
            remote(
                rep.at[h], rep_hbm.at[back, :, pl.ds(h * HALF, HALF)],
                r_s.at[h, k - 1], r_r.at[h, k - 1], {"replica": back},
            ).wait_recv()
    for copy in sent:
        copy.wait_send()
    for copy in outs:
        copy.wait()


def local(cotangent, gate_pre, up_pre, down_weight, projector):
    rows, width = cotangent.shape
    ff = gate_pre.shape[1]
    tokens = rows * lax.axis_size("replica") * lax.axis_size("fsdp")
    scale = 1.0 / math.sqrt(tokens)
    dma = pltpu.SemaphoreType.DMA
    hbm = pl.BlockSpec(memory_space=pl.ANY)
    own, other, parts = pl.pallas_call(
        kernel,
        out_shape=(
            jax.ShapeDtypeStruct((rows, ff), F32),
            jax.ShapeDtypeStruct((rows, ff), BF16),
            jax.ShapeDtypeStruct((NR, 32, ff), BF16),
        ),
        in_specs=[hbm] * 5,
        out_specs=(hbm,) * 3,
        scratch_shapes=[
            pltpu.VMEM((ff, 2048), BF16),
            pltpu.VMEM((2 * rows, 2048), BF16),
            pltpu.VMEM((2, rows, width), BF16),
            pltpu.VMEM((256, width), BF16),
            pltpu.VMEM((rows, ff), BF16),
            pltpu.VMEM((rows, ff), BF16),
            pltpu.VMEM((2, rows, ff), BF16),
            pltpu.VMEM((rows, ff), F32),
            pltpu.VMEM((rows, ff), BF16),
            pltpu.VMEM((NT, 32, 2 * rows), F32),
            pltpu.VMEM((NT - 1, 32, 2 * rows), F32),
            pltpu.VMEM((NT, 32, 2 * rows), BF16),
            pltpu.VMEM((NZ, 32, ff), F32),
            pltpu.VMEM((2, 7, 32, HALF), BF16),
            pltpu.VMEM((2, 7, 32, HALF), BF16),
            pltpu.VMEM((2, 32, HALF), BF16),
            dma((7,)), dma((STREAMS + 2,)),
            dma((2, NM)), dma((2, NM)), dma((2, NM)), dma((2, NM)),
            dma((7,)), dma((7,)), dma((3,)), dma((3,)),
            dma((3, 2, 4)), dma((3, 2, 4)), dma((2,)), dma((2,)),
            dma((7,)), dma((7,)), dma((7,)), dma((7,)),
            dma((2, 7)), dma((2, 7)), dma((2, 3)), dma((2, 3)),
            dma((STREAMS,)), dma((STREAMS,)),
        ],
        compiler_params=pltpu.CompilerParams(
            collective_id=0, has_side_effects=True, vmem_limit_bytes=56000 * 1024
        ),
        name="mlp_backward",
    )(cotangent, gate_pre, up_pre, down_weight, projector.T)

    hidden_grad = own + other.astype(F32)
    gate_float = gate_pre.astype(F32)
    up_float = up_pre.astype(F32)
    sigma = jax.nn.sigmoid(gate_float)
    grad_up = (hidden_grad * (gate_float * sigma)).astype(BF16)
    grad_gate = (hidden_grad * up_float * sigma * (1.0 + gate_float * (1.0 - sigma))).astype(BF16)
    projected_grad = jnp.sum(parts.astype(F32), axis=0) * scale
    return (grad_gate, grad_up, projected_grad)


def solution(mesh):
    placed = (
        P(("replica", "fsdp"), "tensor"),
        P(("replica", "fsdp"), "tensor"),
        P(("replica", "fsdp"), "tensor"),
        P("tensor", "fsdp"),
        P("tensor", "fsdp"),
    )
    return jax.shard_map(
        local,
        mesh=mesh,
        in_specs=placed,
        out_specs=(
            P(("replica", "fsdp"), "tensor"),
            P(("replica", "fsdp"), "tensor"),
            P("fsdp", "tensor"),
        ),
        check_vma=False,
    )
```

```python
import functools
import math

import jax
import jax.numpy as jnp
from jax import lax
from jax.experimental import pallas as pl
from jax.experimental.pallas import tpu as pltpu
from jax.sharding import PartitionSpec as P

F32 = jnp.float32
BF16 = jnp.bfloat16
NZ = 8
NX = 4
NT = 8
NR = 4
FF = 1792
ROWS = 256
STREAMS = FF // ROWS
HALF = FF // 2
LAG = 5
MESSAGES = sorted(
    ((d, i) for i in range(STREAMS) for d in (1, 2, 3, 4)),
    key=lambda m: (2 * m[1] + 3 * m[0], m[1]),
)
NM = len(MESSAGES)
NEAR_FIRST = (1, 7, 2, 6, 3, 5, 4)


def nt_dot(a, b):
    return lax.dot_general(a, b, (((1,), (1,)), ((), ())), preferred_element_type=F32)


def kernel(
    cot_hbm, gate_hbm, up_hbm, w_hbm, pt_hbm, acc_hbm, hx_hbm, rep_hbm,
    wbuf, cotbuf, cot_own, pbuf, gate, up, hidden, acc, hx,
    lr_part, lr_recv, low_rank, pg, ring_send, ring_recv, rep,
    local_sem, out_sem, wz_s, wz_r, ws_s, ws_r, p_s, p_r, sib_s, sib_r,
    own_s, own_r, c_s, c_r, cr_s, cr_r, rs_s, rs_r, ag_s, ag_r, z_s, z_r, r_s, r_r, h_s, h_r,
):
    r = lax.axis_index("replica")
    f = lax.axis_index("fsdp")
    t = lax.axis_index("tensor")
    z, c = f // 2, f % 2
    yl, x = t // NX, t % NX
    par = r % 2
    mate = {"replica": lax.rem(r + 1 - 2 * ((r + c) % 2) + NR, NR)}

    def zdev(k, core=c):
        return {"fsdp": lax.rem(z + k + NZ, NZ) * 2 + core}

    def xdev(k):
        return {"tensor": yl * NX + lax.rem(x + k + NX, NX)}

    sibling = {"fsdp": z * 2 + 1 - c}
    pair = {"tensor": (1 - yl) * NX + x}

    def peer(k):
        return (yl + k // NX) % 2 * NX + (x + k % NX) % NX

    def peer_back(k):
        return (yl + k // NX) % 2 * NX + (x - k % NX + NX) % NX

    def lane(at, size=128):
        return pl.ds(pl.multiple_of(at, 128), size)

    def rows_at(at, size):
        return pl.ds(pl.multiple_of(at, 32), size)

    def remote(src, dst, send, recv, device):
        return pltpu.make_async_remote_copy(
            src_ref=src, dst_ref=dst, send_sem=send, recv_sem=recv,
            device_id=device, device_id_type=pl.DeviceIdType.MESH,
        )

    sent, outs = [], []

    def start(copy):
        copy.start()
        sent.append(copy)

    own_w = wbuf.at[:, lane((z * 2 + c) * 128)]
    loads = [
        pltpu.make_async_copy(pt_hbm, pbuf.at[rows_at(f * 32, 32), :], local_sem.at[0]),
        pltpu.make_async_copy(w_hbm.at[:, lane(par * 128)], own_w, local_sem.at[1]),
        pltpu.make_async_copy(cot_hbm, cot_own.at[c], local_sem.at[2]),
        pltpu.make_async_copy(gate_hbm, gate, local_sem.at[3]),
        pltpu.make_async_copy(up_hbm, up, local_sem.at[4]),
    ]
    loads += [
        pltpu.make_async_copy(
            cot_hbm.at[:, lane(q * 256 + par * 128)],
            cotbuf.at[pl.ds(0, ROWS), lane(t * 256 + q * 128)],
            local_sem.at[5 + q],
        )
        for q in (0, 1)
    ]
    for load in loads:
        load.start()

    barrier = pltpu.get_barrier_semaphore()
    greet = [zdev(k) for k in range(1, NZ)] + [zdev(k, 1 - c) for k in range(NZ)]
    greet += [{"tensor": peer(k)} for k in range(1, NT)]
    greet += [{"replica": lax.rem(r + k, NR)} for k in range(1, NR)]
    greet += [{"replica": lax.rem(r + k, NR), **sibling} for k in range(1, NR)]
    for device in greet:
        pl.semaphore_signal(
            barrier, inc=1, device_id=device, device_id_type=pl.DeviceIdType.MESH
        )
    pl.semaphore_wait(barrier, len(greet))

    def p_copy(core, k, zz):
        ref = pbuf.at[rows_at((zz * 2 + core) * 32, 32), :]
        return remote(ref, ref, p_s.at[core, k], p_r.at[core, k], zdev(k, 1))

    def p_send(core):
        loads[0].wait()
        for k in NEAR_FIRST:
            start(p_copy(core, k, z))
        if core == 0:
            start(p_copy(core, 0, z))

    def chunk(row, xx, j, part=None):
        at = row * NX + lax.rem(xx + NX, NX)
        if part is None:
            return cotbuf.at[pl.ds(j * ROWS, ROWS), lane(at * 256, 256)]
        return cotbuf.at[pl.ds(j * ROWS + part * 128, 128), lane(at * 256, 256)]

    def c_whole(row, j, i):
        ref = chunk(row, x, j)
        for way, sign in ((0, 1), (1, -1)):
            start(remote(ref, ref, c_s.at[i, j, way], c_r.at[i, j, way], xdev(sign)))

    def c_forward(row, j, i):
        for way, sign in ((0, 1), (1, -1)):
            ref = chunk(row, x - sign, j)
            remote(ref, ref, c_s.at[i, j, way], c_r.at[i, j, way], xdev(sign)).wait_recv()
            ref = chunk(row, x - sign, j, way)
            start(remote(
                ref, ref, c_s.at[i, j, 2 + way], c_r.at[i, j, 2 + way], xdev(sign)
            ))

    def c_last(row, j, i):
        for way, sign in ((0, 1), (1, -1)):
            ref = chunk(row, x - 2 * sign, j, way)
            remote(
                ref, ref, c_s.at[i, j, 2 + way], c_r.at[i, j, 2 + way], xdev(sign)
            ).wait_recv()

    def c_pair(j):
        ref = chunk(yl, x, j)
        start(remote(ref, ref, c_s.at[2, j, 0], c_r.at[2, j, 0], pair))

    def c_pair_wait(j):
        ref = chunk(1 - yl, x, j)
        remote(ref, ref, c_s.at[2, j, 0], c_r.at[2, j, 0], pair).wait_recv()

    def c_mate(q):
        return remote(
            cot_own.at[c, :, lane(q * 256 + (1 - par) * 128)],
            cotbuf.at[pl.ds(ROWS, ROWS), lane(t * 256 + q * 128)],
            cr_s.at[q], cr_r.at[q], mate,
        )

    def c_begin():
        loads[2].wait()
        start(c_mate(0))
        start(c_mate(1))
        loads[5].wait()
        loads[6].wait()
        c_pair(0)
        c_whole(yl, 0, 0)

    def w_piece(way, m, zz):
        d, i = MESSAGES[m]
        at, size = (i * ROWS, ROWS) if d < 4 else (i * ROWS + way * 128, 128)
        return wbuf.at[pl.ds(at, size), lane(lax.rem(zz + NZ, NZ) * 256, 256)]

    def w_own(i, core):
        ref = wbuf.at[pl.ds(i * ROWS, ROWS), lane((z * 2 + core) * 128)]
        return remote(ref, ref, own_s.at[core, i], own_r.at[core, i], sibling)

    def needs(m):
        d, i = MESSAGES[m]
        return MESSAGES.index((d - 1, i)) if d > 1 else -1

    def w_send(m):
        d, i = MESSAGES[m]
        if d == 1:
            w_own(i, 1).wait_recv()
        for way, sign in ((0, 1), (1, -1)):
            ref = w_piece(way, m, z - sign * (d - 1))
            start(remote(ref, ref, wz_s.at[way, m], wz_r.at[way, m], zdev(sign)))

    def w_pass(way, m):
        sign = 1 - 2 * way
        ref = w_piece(way, m, z - sign * MESSAGES[m][0])
        return remote(ref, ref, ws_s.at[way, m], ws_r.at[way, m], sibling)

    state = {"sent": 0, "event": 0, "ready": False, "todo": []}

    def w_push(done, lag):
        while state["sent"] < min(NM, done + 1 + lag) and needs(state["sent"]) <= done:
            w_send(state["sent"])
            state["sent"] += 1

    def w_event(lag):
        m = state["event"]
        state["event"] += 1
        d, i = MESSAGES[m]
        for way, sign in ((0, 1), (1, -1)):
            ref = w_piece(way, m, z - sign * d)
            remote(ref, ref, wz_s.at[way, m], wz_r.at[way, m], zdev(sign)).wait_recv()
        w_push(m, lag)
        start(w_pass(0, m))
        start(w_pass(1, m))
        if d == 4:
            state["todo"].append(i)

    def compute(i, core):
        if core == 1:
            w_own(i, 0).wait_recv()
            for m, (_, ii) in enumerate(MESSAGES):
                if ii == i:
                    w_pass(0, m).wait_recv()
                    w_pass(1, m).wait_recv()
        cols = pl.ds(i * ROWS, ROWS)

        def part(j):
            return nt_dot(cotbuf[pl.ds(j * ROWS, ROWS), :], wbuf[cols, :])

        hx[:, cols] = part(1).astype(BF16)
        acc[:, cols] = part(0)
        start(remote(hx.at[:, cols], hx_hbm.at[:, cols], h_s.at[i], h_r.at[i], mate))
        out = pltpu.make_async_copy(acc.at[:, cols], acc_hbm.at[:, cols], out_sem.at[i])
        out.start()
        outs.append(out)

    def pump(events, lag=LAG):
        for _ in range(events):
            if state["event"] < NM:
                w_event(lag)
            if state["ready"] and state["todo"]:
                compute(state["todo"].pop(0), 0)

    def make_hidden(i, carry):
        rows = pl.ds(pl.multiple_of(i * 16, 16), 16)
        g = gate[rows, :].astype(F32)
        activated = g * jax.nn.sigmoid(g)
        hidden[c, rows, :] = (activated * up[rows, :].astype(F32)).astype(BF16)
        return carry

    def hidden_now():
        loads[3].wait()
        loads[4].wait()
        lax.fori_loop(0, 16, make_hidden, 0)

    def to_second(ref, i):
        return remote(ref, ref, sib_s.at[i], sib_r.at[i], sibling)

    def low_rank_part():
        for k in NEAR_FIRST:
            p_copy(0, k, lax.rem(z - k + NZ, NZ)).wait_recv()
            p_copy(1, k, lax.rem(z - k + NZ, NZ)).wait_recv()
        p_copy(0, 0, z).wait_recv()
        to_second(cot_own.at[0], 0).wait_recv()
        part = nt_dot(pbuf[...], cot_own[...].reshape(2 * ROWS, 512))
        lr_part[...] = part.reshape(NT, 64, 2 * ROWS)

    def low_rank_scatter():
        for k in range(1, NT):
            to = peer(k)
            start(remote(
                lr_part.at[to], lr_recv.at[k - 1], rs_s.at[k - 1], rs_r.at[k - 1],
                {"tensor": to},
            ))

    def low_rank_sum():
        total = lr_part[t]
        for k in range(1, NT):
            remote(
                lr_part.at[t], lr_recv.at[k - 1], rs_s.at[k - 1], rs_r.at[k - 1], pair
            ).wait_recv()
            total = total + lr_recv[k - 1]
        low_rank[t] = total.astype(BF16)

    def low_rank_gather():
        for k in range(1, NT):
            ref = low_rank.at[t]
            start(remote(
                ref, ref, ag_s.at[k - 1], ag_r.at[k - 1], {"tensor": peer(k)}
            ))

    def low_rank_wait():
        for k in range(1, NT):
            ref = low_rank.at[peer_back(k)]
            remote(
                ref, ref, ag_s.at[k - 1], ag_r.at[k - 1], {"tensor": peer_back(k)}
            ).wait_recv()

    def grad_tile(n, carry):
        at = lane(n * 256, 256)
        both = jnp.concatenate([hidden[0, :, at], hidden[1, :, at]], axis=0)
        part = jnp.dot(
            low_rank[...].reshape(512, 2 * ROWS), both, preferred_element_type=F32
        )
        pg[:, :, at] = part.reshape(NZ, 64, 256)
        return carry

    def own_part(zz, h):
        return pg[lax.rem(zz + NZ, NZ), :, pl.ds(h * HALF, HALF)]

    def ring(way, step, h):
        i = way * 4 + step
        return remote(
            ring_send.at[h, i], ring_recv.at[h, i], z_s.at[h, i], z_r.at[h, i],
            zdev(1 - 2 * way),
        )

    def ring_step(step, h):
        for way in (0, 1):
            if step < 4 - way:
                i = way * 4 + step
                value = own_part(z + (1 - 2 * way) * (4 - way - step), h)
                if step > 0:
                    ring(way, step - 1, h).wait_recv()
                    value = value + ring_recv[h, i - 1].astype(F32)
                ring_send[h, i] = value.astype(BF16)
        for way in (0, 1):
            if step < 4 - way:
                start(ring(way, step, h))

    def replica_send(h):
        ring(1, 2, h).wait_recv()
        value = own_part(z, h) + ring_recv[h, 6].astype(F32)
        ring(0, 3, h).wait_recv()
        value = value + ring_recv[h, 3].astype(F32)
        rep[h] = value.astype(BF16)
        there = rep_hbm.at[r, :, pl.ds(h * HALF, HALF)]
        for k in range(NR):
            for core in (0, 1):
                mine = rep.at[h, pl.ds(core * 32, 32), :]
                if (k, core) == (0, 1):
                    out = pltpu.make_async_copy(mine, there, out_sem.at[STREAMS + h])
                    out.start()
                    outs.append(out)
                else:
                    start(remote(
                        mine, there, r_s.at[core, h, k], r_r.at[core, h, k],
                        {"replica": lax.rem(r + k, NR), "fsdp": z * 2 + core},
                    ))

    def finish(core):
        for i in range(STREAMS):
            cols = pl.ds(i * ROWS, ROWS)
            remote(
                hx.at[:, cols], hx_hbm.at[:, cols], h_s.at[i], h_r.at[i], mate
            ).wait_recv()
        for h in (0, 1):
            for k in range(core, NR):
                back = lax.rem(r - k + NR, NR)
                remote(
                    rep.at[h, pl.ds(0, 32), :], rep_hbm.at[back, :, pl.ds(h * HALF, HALF)],
                    r_s.at[core, h, k], r_r.at[core, h, k], sibling,
                ).wait_recv()
        for copy in sent:
            copy.wait_send()
        for copy in outs:
            copy.wait()
        sent.clear()
        outs.clear()

    @pl.when(c == 0)
    def _():
        p_send(0)
        loads[1].wait()
        w_push(-1, LAG)
        c_begin()
        start(to_second(cot_own.at[0], 0))
        for i in range(STREAMS):
            start(w_own(i, 0))
        hidden_now()
        start(to_second(hidden.at[0], 1))
        c_pair_wait(0)
        c_whole(1 - yl, 0, 1)
        c_forward(yl, 0, 0)
        pump(1)
        c_mate(0).wait_recv()
        c_mate(1).wait_recv()
        c_pair(1)
        c_whole(yl, 1, 0)
        pump(1)
        c_forward(1 - yl, 0, 1)
        pump(2)
        c_pair_wait(1)
        c_whole(1 - yl, 1, 1)
        c_forward(yl, 1, 0)
        pump(4)
        c_forward(1 - yl, 1, 1)
        pump(2)
        c_last(yl, 0, 0)
        c_last(1 - yl, 0, 1)
        c_last(yl, 1, 0)
        c_last(1 - yl, 1, 1)
        state["ready"] = True
        pump(NM)
        for i in state["todo"]:
            compute(i, 0)
        finish(0)

    @pl.when(c == 1)
    def _():
        loads[1].wait()
        for i in range(STREAMS):
            start(w_own(i, 1))
        p_send(1)
        c_begin()
        hidden_now()
        c_pair_wait(0)
        c_whole(1 - yl, 0, 1)
        c_forward(yl, 0, 0)
        low_rank_part()
        low_rank_scatter()
        c_mate(0).wait_recv()
        c_mate(1).wait_recv()
        c_pair(1)
        c_whole(yl, 1, 0)
        c_forward(1 - yl, 0, 1)
        low_rank_sum()
        low_rank_gather()
        c_pair_wait(1)
        c_whole(1 - yl, 1, 1)
        c_forward(yl, 1, 0)
        low_rank_wait()
        to_second(hidden.at[0], 1).wait_recv()
        lax.fori_loop(0, FF // 256, grad_tile, 0)
        ring_step(0, 0)
        ring_step(0, 1)
        c_forward(1 - yl, 1, 1)
        ring_step(1, 0)
        ring_step(1, 1)
        c_last(yl, 0, 0)
        c_last(1 - yl, 0, 1)
        c_last(yl, 1, 0)
        c_last(1 - yl, 1, 1)
        compute(0, 1)
        ring_step(2, 0)
        ring_step(2, 1)
        compute(1, 1)
        ring_step(3, 0)
        ring_step(3, 1)
        compute(2, 1)
        replica_send(0)
        replica_send(1)
        for i in range(3, STREAMS):
            compute(i, 1)
        finish(1)


def local(cotangent, gate_pre, up_pre, down_weight, projector):
    rows, width = cotangent.shape
    ff = gate_pre.shape[1]
    tokens = rows * lax.axis_size("replica") * lax.axis_size("fsdp")
    scale = 1.0 / math.sqrt(tokens)
    dma = pltpu.SemaphoreType.DMA
    hbm = pl.BlockSpec(memory_space=pl.ANY)
    own, other, parts = pl.pallas_call(
        kernel,
        out_shape=(
            jax.ShapeDtypeStruct((rows, ff), F32),
            jax.ShapeDtypeStruct((rows, ff), BF16),
            jax.ShapeDtypeStruct((NR, 32, ff), BF16),
        ),
        in_specs=[hbm] * 5,
        out_specs=(hbm,) * 3,
        scratch_shapes=[
            pltpu.VMEM((ff, 2048), BF16),
            pltpu.VMEM((2 * rows, 2048), BF16),
            pltpu.VMEM((2, rows, width), BF16),
            pltpu.VMEM((512, width), BF16),
            pltpu.VMEM((rows, ff), BF16),
            pltpu.VMEM((rows, ff), BF16),
            pltpu.VMEM((2, rows, ff), BF16),
            pltpu.VMEM((rows, ff), F32),
            pltpu.VMEM((rows, ff), BF16),
            pltpu.VMEM((NT, 64, 2 * rows), F32),
            pltpu.VMEM((NT - 1, 64, 2 * rows), F32),
            pltpu.VMEM((NT, 64, 2 * rows), BF16),
            pltpu.VMEM((NZ, 64, ff), F32),
            pltpu.VMEM((2, 7, 64, HALF), BF16),
            pltpu.VMEM((2, 7, 64, HALF), BF16),
            pltpu.VMEM((2, 64, HALF), BF16),
            dma((7,)), dma((STREAMS + 2,)),
            dma((2, NM)), dma((2, NM)), dma((2, NM)), dma((2, NM)),
            dma((2, NZ)), dma((2, NZ)), dma((2,)), dma((2,)),
            dma((2, STREAMS)), dma((2, STREAMS)),
            dma((3, 2, 4)), dma((3, 2, 4)), dma((2,)), dma((2,)),
            dma((7,)), dma((7,)), dma((7,)), dma((7,)),
            dma((2, 7)), dma((2, 7)), dma((2, 2, NR)), dma((2, 2, NR)),
            dma((STREAMS,)), dma((STREAMS,)),
        ],
        compiler_params=pltpu.CompilerParams(
            collective_id=0, has_side_effects=True, vmem_limit_bytes=56000 * 1024
        ),
        name="mlp_backward",
    )(cotangent, gate_pre, up_pre, down_weight, projector.T)

    hidden_grad = own + other.astype(F32)
    gate_float = gate_pre.astype(F32)
    up_float = up_pre.astype(F32)
    sigma = jax.nn.sigmoid(gate_float)
    grad_up = (hidden_grad * (gate_float * sigma)).astype(BF16)
    grad_gate = (hidden_grad * up_float * sigma * (1.0 + gate_float * (1.0 - sigma))).astype(BF16)
    projected_grad = jnp.sum(parts.astype(F32), axis=0) * scale
    return (grad_gate, grad_up, projected_grad)


def solution(mesh):
    placed = (
        P(("replica", "fsdp"), "tensor"),
        P(("replica", "fsdp"), "tensor"),
        P(("replica", "fsdp"), "tensor"),
        P("tensor", "fsdp"),
        P("tensor", "fsdp"),
    )
    return jax.shard_map(
        local,
        mesh=mesh,
        in_specs=placed,
        out_specs=(
            P(("replica", "fsdp"), "tensor"),
            P(("replica", "fsdp"), "tensor"),
            P("fsdp", "tensor"),
        ),
        check_vma=False,
    )
```

```python
import functools
import math

import jax
import jax.numpy as jnp
from jax import lax
from jax.experimental import pallas as pl
from jax.experimental.pallas import tpu as pltpu
from jax.sharding import PartitionSpec as P

F32 = jnp.float32
BF16 = jnp.bfloat16
NZ = 8
NX = 4
NT = 8
NR = 4
FF = 1792
ROWS = 256
STREAMS = FF // ROWS
HALF = FF // 2
LAG = 5
MESSAGES = sorted(
    ((d, i) for i in range(STREAMS) for d in (1, 2, 3, 4)),
    key=lambda m: (2 * m[1] + 3 * m[0], m[1]),
)
NM = len(MESSAGES)
NEAR_FIRST = (1, 7, 2, 6, 3, 5, 4)


def nt_dot(a, b):
    return lax.dot_general(a, b, (((1,), (1,)), ((), ())), preferred_element_type=F32)


def kernel(
    cot_hbm, gate_hbm, up_hbm, w_hbm, pt_hbm, gg_hbm, gu_hbm, rep_hbm,
    wbuf, cotbuf, cot_own, pbuf, gate, up, act, factor, hidden, acc, hx, hx_in, gg, gu,
    lr_full, lr_part, lr_recv, low_rank, pg, ring_send, ring_recv, rep,
    local_sem, out_sem, wz_s, wz_r, ws_s, ws_r, p_s, p_r, sib_s, sib_r,
    own_s, own_r, c_s, c_r, cr_s, cr_r, rs_s, rs_r, ag_s, ag_r, z_s, z_r, r_s, r_r, h_s, h_r,
):
    r = lax.axis_index("replica")
    f = lax.axis_index("fsdp")
    t = lax.axis_index("tensor")
    z, c = f // 2, f % 2
    yl, x = t // NX, t % NX
    par = r % 2
    mate = {"replica": lax.rem(r + 1 - 2 * ((r + c) % 2) + NR, NR)}

    def zdev(k, core=c):
        return {"fsdp": lax.rem(z + k + NZ, NZ) * 2 + core}

    def xdev(k):
        return {"tensor": yl * NX + lax.rem(x + k + NX, NX)}

    sibling = {"fsdp": z * 2 + 1 - c}
    pair = {"tensor": (1 - yl) * NX + x}

    def peer(k):
        return (yl + k // NX) % 2 * NX + (x + k % NX) % NX

    def peer_back(k):
        return (yl + k // NX) % 2 * NX + (x - k % NX + NX) % NX

    def lane(at, size=128):
        return pl.ds(pl.multiple_of(at, 128), size)

    def rows_at(at, size):
        return pl.ds(pl.multiple_of(at, 32), size)

    def remote(src, dst, send, recv, device):
        return pltpu.make_async_remote_copy(
            src_ref=src, dst_ref=dst, send_sem=send, recv_sem=recv,
            device_id=device, device_id_type=pl.DeviceIdType.MESH,
        )

    sent, outs = [], []

    def start(copy):
        copy.start()
        sent.append(copy)

    own_w = wbuf.at[:, lane((z * 2 + c) * 128)]
    loads = [
        pltpu.make_async_copy(pt_hbm, pbuf.at[rows_at(f * 32, 32), :], local_sem.at[0]),
        pltpu.make_async_copy(w_hbm.at[:, lane(par * 128)], own_w, local_sem.at[1]),
        pltpu.make_async_copy(cot_hbm, cot_own.at[c], local_sem.at[2]),
        pltpu.make_async_copy(gate_hbm, gate, local_sem.at[3]),
        pltpu.make_async_copy(up_hbm, up, local_sem.at[4]),
    ]
    loads += [
        pltpu.make_async_copy(
            cot_hbm.at[:, lane(q * 256 + par * 128)],
            cotbuf.at[pl.ds(0, ROWS), lane(t * 256 + q * 128)],
            local_sem.at[5 + q],
        )
        for q in (0, 1)
    ]
    for load in loads:
        load.start()

    barrier = pltpu.get_barrier_semaphore()
    greet = [zdev(k) for k in range(1, NZ)] + [zdev(k, 1 - c) for k in range(NZ)]
    greet += [{"tensor": peer(k)} for k in range(1, NT)]
    greet += [{"replica": lax.rem(r + k, NR)} for k in range(1, NR)]
    greet += [{"replica": lax.rem(r + k, NR), **sibling} for k in range(1, NR)]
    for device in greet:
        pl.semaphore_signal(
            barrier, inc=1, device_id=device, device_id_type=pl.DeviceIdType.MESH
        )
    pl.semaphore_wait(barrier, len(greet))

    def p_copy(core, k, zz):
        ref = pbuf.at[rows_at((zz * 2 + core) * 32, 32), :]
        return remote(ref, ref, p_s.at[core, k], p_r.at[core, k], zdev(k, 1))

    def p_send(core):
        loads[0].wait()
        for k in NEAR_FIRST:
            start(p_copy(core, k, z))
        if core == 0:
            start(p_copy(core, 0, z))

    def chunk(row, xx, j, part=None):
        at = row * NX + lax.rem(xx + NX, NX)
        if part is None:
            return cotbuf.at[pl.ds(j * ROWS, ROWS), lane(at * 256, 256)]
        return cotbuf.at[pl.ds(j * ROWS + part * 128, 128), lane(at * 256, 256)]

    def c_whole(row, j, i):
        ref = chunk(row, x, j)
        for way, sign in ((0, 1), (1, -1)):
            start(remote(ref, ref, c_s.at[i, j, way], c_r.at[i, j, way], xdev(sign)))

    def c_forward(row, j, i):
        for way, sign in ((0, 1), (1, -1)):
            ref = chunk(row, x - sign, j)
            remote(ref, ref, c_s.at[i, j, way], c_r.at[i, j, way], xdev(sign)).wait_recv()
            ref = chunk(row, x - sign, j, way)
            start(remote(
                ref, ref, c_s.at[i, j, 2 + way], c_r.at[i, j, 2 + way], xdev(sign)
            ))

    def c_last(row, j, i):
        for way, sign in ((0, 1), (1, -1)):
            ref = chunk(row, x - 2 * sign, j, way)
            remote(
                ref, ref, c_s.at[i, j, 2 + way], c_r.at[i, j, 2 + way], xdev(sign)
            ).wait_recv()

    def c_pair(j):
        ref = chunk(yl, x, j)
        start(remote(ref, ref, c_s.at[2, j, 0], c_r.at[2, j, 0], pair))

    def c_pair_wait(j):
        ref = chunk(1 - yl, x, j)
        remote(ref, ref, c_s.at[2, j, 0], c_r.at[2, j, 0], pair).wait_recv()

    def c_mate(q):
        return remote(
            cot_own.at[c, :, lane(q * 256 + (1 - par) * 128)],
            cotbuf.at[pl.ds(ROWS, ROWS), lane(t * 256 + q * 128)],
            cr_s.at[q], cr_r.at[q], mate,
        )

    def c_begin():
        loads[2].wait()
        start(c_mate(0))
        start(c_mate(1))
        loads[5].wait()
        loads[6].wait()
        c_pair(0)
        c_whole(yl, 0, 0)

    def c_mates():
        c_mate(0).wait_recv()
        c_mate(1).wait_recv()
        c_pair(1)
        c_whole(yl, 1, 0)

    def w_piece(way, m, zz):
        d, i = MESSAGES[m]
        at, size = (i * ROWS, ROWS) if d < 4 else (i * ROWS + way * 128, 128)
        return wbuf.at[pl.ds(at, size), lane(lax.rem(zz + NZ, NZ) * 256, 256)]

    def w_own(i, core):
        ref = wbuf.at[pl.ds(i * ROWS, ROWS), lane((z * 2 + core) * 128)]
        return remote(ref, ref, own_s.at[core, i], own_r.at[core, i], sibling)

    def needs(m):
        d, i = MESSAGES[m]
        return MESSAGES.index((d - 1, i)) if d > 1 else -1

    def w_send(m):
        d, i = MESSAGES[m]
        if d == 1:
            w_own(i, 1).wait_recv()
        for way, sign in ((0, 1), (1, -1)):
            ref = w_piece(way, m, z - sign * (d - 1))
            start(remote(ref, ref, wz_s.at[way, m], wz_r.at[way, m], zdev(sign)))

    def w_pass(way, m):
        sign = 1 - 2 * way
        ref = w_piece(way, m, z - sign * MESSAGES[m][0])
        return remote(ref, ref, ws_s.at[way, m], ws_r.at[way, m], sibling)

    state = {"sent": 0, "event": 0, "ready": False, "todo": [], "whole": False, "own": []}

    def w_push(done, lag):
        while state["sent"] < min(NM, done + 1 + lag) and needs(state["sent"]) <= done:
            w_send(state["sent"])
            state["sent"] += 1

    def w_event(lag):
        m = state["event"]
        state["event"] += 1
        d, i = MESSAGES[m]
        for way, sign in ((0, 1), (1, -1)):
            ref = w_piece(way, m, z - sign * d)
            remote(ref, ref, wz_s.at[way, m], wz_r.at[way, m], zdev(sign)).wait_recv()
        w_push(m, lag)
        start(w_pass(0, m))
        start(w_pass(1, m))
        if d == 4:
            state["todo"].append(i)

    def part(j, i):
        cols = pl.ds(i * ROWS, ROWS)
        return nt_dot(cotbuf[pl.ds(j * ROWS, ROWS), :], wbuf[cols, :])

    def mates(i, core):
        if core == 1:
            w_own(i, 0).wait_recv()
            for m, (_, ii) in enumerate(MESSAGES):
                if ii == i:
                    w_pass(0, m).wait_recv()
                    w_pass(1, m).wait_recv()
        cols = pl.ds(i * ROWS, ROWS)
        hx[:, cols] = part(1, i).astype(BF16)
        start(remote(hx.at[:, cols], hx_in.at[:, cols], h_s.at[i], h_r.at[i], mate))

    def own(i):
        acc[:, pl.ds(i * ROWS, ROWS)] = part(0, i)

    def gradients(i):
        cols = pl.ds(i * ROWS, ROWS)
        remote(hx.at[:, cols], hx_in.at[:, cols], h_s.at[i], h_r.at[i], mate).wait_recv()
        total = acc[:, cols] + hx_in[:, cols].astype(F32)
        gg[:, cols] = (total * factor[:, cols]).astype(BF16)
        gu[:, cols] = (total * act[:, cols]).astype(BF16)
        for n, (here, there) in enumerate(((gg, gg_hbm), (gu, gu_hbm))):
            out = pltpu.make_async_copy(
                here.at[:, cols], there.at[:, cols], out_sem.at[2 * i + n]
            )
            out.start()
            outs.append(out)

    def pump(events, lag=LAG):
        for _ in range(events):
            if state["event"] < NM:
                w_event(lag)
            if state["ready"] and state["todo"]:
                i = state["todo"].pop(0)
                mates(i, 0)
                state["own"].append(i)
            elif state["whole"] and state["own"]:
                i = state["own"].pop(0)
                own(i)
                if i > 1:
                    gradients(i - 2)

    def make_hidden(i, carry):
        rows = pl.ds(pl.multiple_of(i * 16, 16), 16)
        g = gate[rows, :].astype(F32)
        u = up[rows, :].astype(F32)
        sigma = jax.nn.sigmoid(g)
        activated = g * sigma
        act[rows, :] = activated
        factor[rows, :] = u * sigma * (1.0 + g * (1.0 - sigma))
        hidden[c, rows, :] = (activated * u).astype(BF16)
        return carry

    def hidden_now():
        loads[3].wait()
        loads[4].wait()
        lax.fori_loop(0, 16, make_hidden, 0)

    def to_second(ref, i):
        return remote(ref, ref, sib_s.at[i], sib_r.at[i], sibling)

    def low_rank_part():
        for k in NEAR_FIRST:
            p_copy(0, k, lax.rem(z - k + NZ, NZ)).wait_recv()
            p_copy(1, k, lax.rem(z - k + NZ, NZ)).wait_recv()
        p_copy(0, 0, z).wait_recv()
        to_second(cot_own.at[0], 0).wait_recv()
        part = nt_dot(pbuf[...], cot_own[...].reshape(2 * ROWS, 512))
        part = part.reshape(NT, 64, 2 * ROWS)
        lr_full[...] = part
        lr_part[...] = part.astype(BF16)

    def low_rank_scatter():
        for k in range(1, NT):
            to = peer(k)
            start(remote(
                lr_part.at[to], lr_recv.at[k - 1], rs_s.at[k - 1], rs_r.at[k - 1],
                {"tensor": to},
            ))

    def low_rank_sum():
        total = lr_full[t]
        for k in range(1, NT):
            remote(
                lr_part.at[t], lr_recv.at[k - 1], rs_s.at[k - 1], rs_r.at[k - 1], pair
            ).wait_recv()
            total = total + lr_recv[k - 1].astype(F32)
        low_rank[t] = total.astype(BF16)

    def low_rank_gather():
        for k in range(1, NT):
            ref = low_rank.at[t]
            start(remote(
                ref, ref, ag_s.at[k - 1], ag_r.at[k - 1], {"tensor": peer(k)}
            ))

    def low_rank_wait():
        for k in range(1, NT):
            ref = low_rank.at[peer_back(k)]
            remote(
                ref, ref, ag_s.at[k - 1], ag_r.at[k - 1], {"tensor": peer_back(k)}
            ).wait_recv()

    def grad_tile(n, carry):
        at = lane(n * 256, 256)
        both = jnp.concatenate([hidden[0, :, at], hidden[1, :, at]], axis=0)
        part = jnp.dot(
            low_rank[...].reshape(512, 2 * ROWS), both, preferred_element_type=F32
        )
        pg[:, :, at] = part.reshape(NZ, 64, 256)
        return carry

    def own_part(zz, h):
        return pg[lax.rem(zz + NZ, NZ), :, pl.ds(h * HALF, HALF)]

    def ring(way, step, h):
        i = way * 4 + step
        return remote(
            ring_send.at[h, i], ring_recv.at[h, i], z_s.at[h, i], z_r.at[h, i],
            zdev(1 - 2 * way),
        )

    def ring_step(step, h):
        for way in (0, 1):
            if step < 4 - way:
                i = way * 4 + step
                value = own_part(z + (1 - 2 * way) * (4 - way - step), h)
                if step > 0:
                    ring(way, step - 1, h).wait_recv()
                    value = value + ring_recv[h, i - 1].astype(F32)
                ring_send[h, i] = value.astype(BF16)
        for way in (0, 1):
            if step < 4 - way:
                start(ring(way, step, h))

    def replica_send(h):
        ring(1, 2, h).wait_recv()
        value = own_part(z, h) + ring_recv[h, 6].astype(F32)
        ring(0, 3, h).wait_recv()
        value = value + ring_recv[h, 3].astype(F32)
        rep[h] = value.astype(BF16)
        there = rep_hbm.at[r, :, pl.ds(h * HALF, HALF)]
        for k in range(NR):
            for core in (0, 1):
                mine = rep.at[h, pl.ds(core * 32, 32), :]
                if (k, core) == (0, 1):
                    out = pltpu.make_async_copy(mine, there, out_sem.at[2 * STREAMS + h])
                    out.start()
                    outs.append(out)
                else:
                    start(remote(
                        mine, there, r_s.at[core, h, k], r_r.at[core, h, k],
                        {"replica": lax.rem(r + k, NR), "fsdp": z * 2 + core},
                    ))

    def finish(core):
        for i in range(STREAMS - 2, STREAMS):
            gradients(i)
        for h in (0, 1):
            for k in range(core, NR):
                back = lax.rem(r - k + NR, NR)
                remote(
                    rep.at[h, pl.ds(0, 32), :], rep_hbm.at[back, :, pl.ds(h * HALF, HALF)],
                    r_s.at[core, h, k], r_r.at[core, h, k], sibling,
                ).wait_recv()
        for copy in sent:
            copy.wait_send()
        for copy in outs:
            copy.wait()
        sent.clear()
        outs.clear()

    @pl.when(c == 0)
    def _():
        p_send(0)
        c_begin()
        start(to_second(cot_own.at[0], 0))
        loads[1].wait()
        for i in range(STREAMS):
            start(w_own(i, 0))
        hidden_now()
        start(to_second(hidden.at[0], 1))
        w_push(-1, LAG)
        c_mates()
        pump(1)
        c_pair_wait(1)
        c_whole(1 - yl, 1, 1)
        c_forward(yl, 1, 0)
        pump(3)
        c_forward(1 - yl, 1, 1)
        pump(3)
        c_last(yl, 1, 0)
        c_last(1 - yl, 1, 1)
        state["ready"] = True
        c_pair_wait(0)
        c_whole(1 - yl, 0, 1)
        c_forward(yl, 0, 0)
        pump(4)
        c_forward(1 - yl, 0, 1)
        pump(4)
        c_last(yl, 0, 0)
        c_last(1 - yl, 0, 1)
        state["whole"] = True
        pump(NM)
        assert not state["todo"] and not state["own"]
        finish(0)

    @pl.when(c == 1)
    def _():
        loads[1].wait()
        for i in range(STREAMS):
            start(w_own(i, 1))
        p_send(1)
        c_begin()
        hidden_now()
        c_mates()
        low_rank_part()
        low_rank_scatter()
        c_pair_wait(1)
        c_whole(1 - yl, 1, 1)
        c_forward(yl, 1, 0)
        low_rank_sum()
        low_rank_gather()
        c_forward(1 - yl, 1, 1)
        c_pair_wait(0)
        c_whole(1 - yl, 0, 1)
        c_forward(yl, 0, 0)
        low_rank_wait()
        to_second(hidden.at[0], 1).wait_recv()
        lax.fori_loop(0, FF // 256, grad_tile, 0)
        ring_step(0, 0)
        ring_step(0, 1)
        c_last(yl, 1, 0)
        c_last(1 - yl, 1, 1)
        c_forward(1 - yl, 0, 1)
        mates(0, 1)
        ring_step(1, 0)
        ring_step(1, 1)
        c_last(yl, 0, 0)
        c_last(1 - yl, 0, 1)
        own(0)
        ring_step(2, 0)
        ring_step(2, 1)
        mates(1, 1)
        ring_step(3, 0)
        ring_step(3, 1)
        mates(2, 1)
        replica_send(0)
        replica_send(1)
        own(1)
        for i in range(3, STREAMS):
            mates(i, 1)
            own(i - 1)
            gradients(i - 3)
        own(STREAMS - 1)
        gradients(STREAMS - 3)
        finish(1)


def tail(scale, gg_in, gu_in, parts_in, gg, gu, pg, gg_v, gu_v, parts_v, pg_v, sems):
    quarters = []
    for n, (here, buffer, there) in enumerate(((gg_in, gg_v, gg), (gu_in, gu_v, gu))):
        for q in range(4):
            rows = pl.ds(q * 64, 64)
            i = n * 4 + q
            quarters.append((
                pltpu.make_async_copy(here.at[rows], buffer.at[rows], sems.at[0, i]),
                pltpu.make_async_copy(buffer.at[rows], there.at[rows], sems.at[1, i]),
            ))
    parts = pltpu.make_async_copy(parts_in, parts_v, sems.at[0, 8])
    result = pltpu.make_async_copy(pg_v, pg, sems.at[1, 8])
    parts.start()
    for load, _ in quarters:
        load.start()
    parts.wait()
    total = parts_v[0].astype(F32)
    for k in range(1, NR):
        total = total + parts_v[k].astype(F32)
    pg_v[...] = total * scale
    result.start()
    for load, store in quarters:
        load.wait()
        store.start()
    for _, store in quarters:
        store.wait()
    result.wait()


def local(cotangent, gate_pre, up_pre, down_weight, projector):
    rows, width = cotangent.shape
    ff = gate_pre.shape[1]
    tokens = rows * lax.axis_size("replica") * lax.axis_size("fsdp")
    scale = 1.0 / math.sqrt(tokens)
    dma = pltpu.SemaphoreType.DMA
    hbm = pl.BlockSpec(memory_space=pl.ANY)
    grad_gate, grad_up, parts = pl.pallas_call(
        kernel,
        out_shape=(
            jax.ShapeDtypeStruct((rows, ff), BF16),
            jax.ShapeDtypeStruct((rows, ff), BF16),
            jax.ShapeDtypeStruct((NR, 32, ff), BF16),
        ),
        in_specs=[hbm] * 5,
        out_specs=(hbm,) * 3,
        scratch_shapes=[
            pltpu.VMEM((ff, 2048), BF16),
            pltpu.VMEM((2 * rows, 2048), BF16),
            pltpu.VMEM((2, rows, width), BF16),
            pltpu.VMEM((512, width), BF16),
            pltpu.VMEM((rows, ff), BF16),
            pltpu.VMEM((rows, ff), BF16),
            pltpu.VMEM((rows, ff), F32),
            pltpu.VMEM((rows, ff), F32),
            pltpu.VMEM((2, rows, ff), BF16),
            pltpu.VMEM((rows, ff), F32),
            pltpu.VMEM((rows, ff), BF16),
            pltpu.VMEM((rows, ff), BF16),
            pltpu.VMEM((rows, ff), BF16),
            pltpu.VMEM((rows, ff), BF16),
            pltpu.VMEM((NT, 64, 2 * rows), F32),
            pltpu.VMEM((NT, 64, 2 * rows), BF16),
            pltpu.VMEM((NT - 1, 64, 2 * rows), BF16),
            pltpu.VMEM((NT, 64, 2 * rows), BF16),
            pltpu.VMEM((NZ, 64, ff), F32),
            pltpu.VMEM((2, 7, 64, HALF), BF16),
            pltpu.VMEM((2, 7, 64, HALF), BF16),
            pltpu.VMEM((2, 64, HALF), BF16),
            dma((7,)), dma((2 * STREAMS + 2,)),
            dma((2, NM)), dma((2, NM)), dma((2, NM)), dma((2, NM)),
            dma((2, NZ)), dma((2, NZ)), dma((2,)), dma((2,)),
            dma((2, STREAMS)), dma((2, STREAMS)),
            dma((3, 2, 4)), dma((3, 2, 4)), dma((2,)), dma((2,)),
            dma((7,)), dma((7,)), dma((7,)), dma((7,)),
            dma((2, 7)), dma((2, 7)), dma((2, 2, NR)), dma((2, 2, NR)),
            dma((STREAMS,)), dma((STREAMS,)),
        ],
        compiler_params=pltpu.CompilerParams(
            collective_id=0, has_side_effects=True, vmem_limit_bytes=56000 * 1024
        ),
        name="mlp_backward",
    )(cotangent, gate_pre, up_pre, down_weight, projector.T)

    return pl.pallas_call(
        functools.partial(tail, scale),
        out_shape=(
            jax.ShapeDtypeStruct((rows, ff), BF16),
            jax.ShapeDtypeStruct((rows, ff), BF16),
            jax.ShapeDtypeStruct((32, ff), F32),
        ),
        in_specs=[hbm] * 3,
        out_specs=(hbm,) * 3,
        scratch_shapes=[
            pltpu.VMEM((rows, ff), BF16),
            pltpu.VMEM((rows, ff), BF16),
            pltpu.VMEM((NR, 32, ff), BF16),
            pltpu.VMEM((32, ff), F32),
            dma((2, 9)),
        ],
        name="outputs",
    )(grad_gate, grad_up, parts)


def solution(mesh):
    placed = (
        P(("replica", "fsdp"), "tensor"),
        P(("replica", "fsdp"), "tensor"),
        P(("replica", "fsdp"), "tensor"),
        P("tensor", "fsdp"),
        P("tensor", "fsdp"),
    )
    return jax.shard_map(
        local,
        mesh=mesh,
        in_specs=placed,
        out_specs=(
            P(("replica", "fsdp"), "tensor"),
            P(("replica", "fsdp"), "tensor"),
            P("fsdp", "tensor"),
        ),
        check_vma=False,
    )
```

```python
import functools
import math

import jax
import jax.numpy as jnp
from jax import lax
from jax.experimental import pallas as pl
from jax.experimental.pallas import tpu as pltpu
from jax.sharding import PartitionSpec as P

F32 = jnp.float32
BF16 = jnp.bfloat16
NZ = 8
NX = 4
NT = 8
NR = 4
FF = 1792
ROWS = 256
STREAMS = FF // ROWS
HALF = FF // 2
LAG = 5
MESSAGES = sorted(
    ((d, i) for i in range(STREAMS) for d in (1, 2, 3, 4)),
    key=lambda m: (2 * m[1] + 3 * m[0], m[1]),
)
NM = len(MESSAGES)


def nt_dot(a, b):
    return lax.dot_general(a, b, (((1,), (1,)), ((), ())), preferred_element_type=F32)


def kernel(
    cot_hbm, gate_hbm, up_hbm, w_hbm, pt_hbm, gg_hbm, gu_hbm, rep_hbm,
    wbuf, cotbuf, cot_own, pbuf, gate, up, act, factor, hidden, acc, hx, hx_in, gg, gu,
    lr_full, lr_part, lr_recv, low_rank, pg, ring_send, ring_recv, rep,
    local_sem, out_sem, wz_s, wz_r, ws_s, ws_r, p_s, p_r, sib_s, sib_r,
    own_s, own_r, c_s, c_r, cr_s, cr_r, rs_s, rs_r, ag_s, ag_r, z_s, z_r, r_s, r_r, h_s, h_r,
):
    r = lax.axis_index("replica")
    f = lax.axis_index("fsdp")
    t = lax.axis_index("tensor")
    z, c = f // 2, f % 2
    yl, x = t // NX, t % NX
    par = r % 2
    mate = {"replica": lax.rem(r + 1 - 2 * ((r + c) % 2) + NR, NR)}

    def zdev(k, core=c):
        return {"fsdp": lax.rem(z + k + NZ, NZ) * 2 + core}

    def xdev(k):
        return {"tensor": yl * NX + lax.rem(x + k + NX, NX)}

    sibling = {"fsdp": z * 2 + 1 - c}
    pair = {"tensor": (1 - yl) * NX + x}

    def peer(k):
        return (yl + k // NX) % 2 * NX + (x + k % NX) % NX

    def peer_back(k):
        return (yl + k // NX) % 2 * NX + (x - k % NX + NX) % NX

    def lane(at, size=128):
        return pl.ds(pl.multiple_of(at, 128), size)

    def rows_at(at, size):
        return pl.ds(pl.multiple_of(at, 32), size)

    def remote(src, dst, send, recv, device):
        return pltpu.make_async_remote_copy(
            src_ref=src, dst_ref=dst, send_sem=send, recv_sem=recv,
            device_id=device, device_id_type=pl.DeviceIdType.MESH,
        )

    sent, outs = [], []

    def start(copy):
        copy.start()
        sent.append(copy)

    own_w = wbuf.at[:, lane((z * 2 + c) * 128)]
    loads = [
        pltpu.make_async_copy(pt_hbm, pbuf.at[rows_at(f * 32, 32), :], local_sem.at[0]),
        pltpu.make_async_copy(w_hbm.at[:, lane(par * 128)], own_w, local_sem.at[1]),
        pltpu.make_async_copy(cot_hbm, cot_own.at[c], local_sem.at[2]),
        pltpu.make_async_copy(gate_hbm, gate, local_sem.at[3]),
        pltpu.make_async_copy(up_hbm, up, local_sem.at[4]),
    ]
    loads += [
        pltpu.make_async_copy(
            cot_hbm.at[:, lane(q * 256 + par * 128)],
            cotbuf.at[pl.ds(0, ROWS), lane(t * 256 + q * 128)],
            local_sem.at[5 + q],
        )
        for q in (0, 1)
    ]
    for load in loads:
        load.start()

    barrier = pltpu.get_barrier_semaphore()
    greet = [zdev(k) for k in range(1, NZ)] + [zdev(k, 1 - c) for k in range(NZ)]
    greet += [{"tensor": peer(k)} for k in range(1, NT)]
    greet += [{"replica": lax.rem(r + k, NR)} for k in range(1, NR)]
    greet += [{"replica": lax.rem(r + k, NR), **sibling} for k in range(1, NR)]
    for device in greet:
        pl.semaphore_signal(
            barrier, inc=1, device_id=device, device_id_type=pl.DeviceIdType.MESH
        )
    pl.semaphore_wait(barrier, len(greet))

    def p_pass(core_rows, size, device, way, d):
        ref = pbuf.at[rows_at(core_rows, size), :]
        return remote(ref, ref, p_s.at[way, d], p_r.at[way, d], device)

    def p_hop(way, d, behind):
        sign = 1 - 2 * way
        at = lax.rem(z - sign * behind + NZ, NZ)
        return p_pass(at * 64, 64, zdev(sign), way, d)

    def p_relay(d):
        for way in (0, 1):
            if d <= 4 - way:
                if d > 0:
                    p_hop(way, d, d).wait_recv()
                if d + 1 <= 4 - way:
                    start(p_hop(way, d + 1, d))

    def chunk(row, xx, j, part=None):
        at = row * NX + lax.rem(xx + NX, NX)
        if part is None:
            return cotbuf.at[pl.ds(j * ROWS, ROWS), lane(at * 256, 256)]
        return cotbuf.at[pl.ds(j * ROWS + part * 128, 128), lane(at * 256, 256)]

    def c_whole(row, j, i):
        ref = chunk(row, x, j)
        for way, sign in ((0, 1), (1, -1)):
            start(remote(ref, ref, c_s.at[i, j, way], c_r.at[i, j, way], xdev(sign)))

    def c_forward(row, j, i):
        for way, sign in ((0, 1), (1, -1)):
            ref = chunk(row, x - sign, j)
            remote(ref, ref, c_s.at[i, j, way], c_r.at[i, j, way], xdev(sign)).wait_recv()
            ref = chunk(row, x - sign, j, way)
            start(remote(
                ref, ref, c_s.at[i, j, 2 + way], c_r.at[i, j, 2 + way], xdev(sign)
            ))

    def c_last(row, j, i):
        for way, sign in ((0, 1), (1, -1)):
            ref = chunk(row, x - 2 * sign, j, way)
            remote(
                ref, ref, c_s.at[i, j, 2 + way], c_r.at[i, j, 2 + way], xdev(sign)
            ).wait_recv()

    def c_pair(j):
        ref = chunk(yl, x, j)
        start(remote(ref, ref, c_s.at[2, j, 0], c_r.at[2, j, 0], pair))

    def c_pair_wait(j):
        ref = chunk(1 - yl, x, j)
        remote(ref, ref, c_s.at[2, j, 0], c_r.at[2, j, 0], pair).wait_recv()

    def c_mate(q):
        return remote(
            cot_own.at[c, :, lane(q * 256 + (1 - par) * 128)],
            cotbuf.at[pl.ds(ROWS, ROWS), lane(t * 256 + q * 128)],
            cr_s.at[q], cr_r.at[q], mate,
        )

    def c_begin():
        loads[2].wait()
        start(c_mate(0))
        start(c_mate(1))
        loads[5].wait()
        loads[6].wait()
        c_pair(0)
        c_whole(yl, 0, 0)

    def c_mates():
        c_mate(0).wait_recv()
        c_mate(1).wait_recv()
        c_pair(1)
        c_whole(yl, 1, 0)

    def w_piece(way, m, zz):
        d, i = MESSAGES[m]
        at, size = (i * ROWS, ROWS) if d < 4 else (i * ROWS + way * 128, 128)
        return wbuf.at[pl.ds(at, size), lane(lax.rem(zz + NZ, NZ) * 256, 256)]

    def w_own(i, core):
        ref = wbuf.at[pl.ds(i * ROWS, ROWS), lane((z * 2 + core) * 128)]
        return remote(ref, ref, own_s.at[core, i], own_r.at[core, i], sibling)

    def needs(m):
        d, i = MESSAGES[m]
        return MESSAGES.index((d - 1, i)) if d > 1 else -1

    def w_send(m):
        d, i = MESSAGES[m]
        if d == 1:
            w_own(i, 1).wait_recv()
        for way, sign in ((0, 1), (1, -1)):
            ref = w_piece(way, m, z - sign * (d - 1))
            start(remote(ref, ref, wz_s.at[way, m], wz_r.at[way, m], zdev(sign)))

    def w_pass(way, m):
        sign = 1 - 2 * way
        ref = w_piece(way, m, z - sign * MESSAGES[m][0])
        return remote(ref, ref, ws_s.at[way, m], ws_r.at[way, m], sibling)

    state = {"sent": 0, "event": 0, "ready": False, "todo": [], "whole": False, "own": []}

    def w_push(done, lag):
        while state["sent"] < min(NM, done + 1 + lag) and needs(state["sent"]) <= done:
            w_send(state["sent"])
            state["sent"] += 1

    def w_event(lag):
        m = state["event"]
        state["event"] += 1
        d, i = MESSAGES[m]
        for way, sign in ((0, 1), (1, -1)):
            ref = w_piece(way, m, z - sign * d)
            remote(ref, ref, wz_s.at[way, m], wz_r.at[way, m], zdev(sign)).wait_recv()
        w_push(m, lag)
        start(w_pass(0, m))
        start(w_pass(1, m))
        if d == 4:
            state["todo"].append(i)

    def part(j, i):
        cols = pl.ds(i * ROWS, ROWS)
        return nt_dot(cotbuf[pl.ds(j * ROWS, ROWS), :], wbuf[cols, :])

    def mates(i, core):
        if core == 1:
            w_own(i, 0).wait_recv()
            for m, (_, ii) in enumerate(MESSAGES):
                if ii == i:
                    w_pass(0, m).wait_recv()
                    w_pass(1, m).wait_recv()
        cols = pl.ds(i * ROWS, ROWS)
        hx[:, cols] = part(1, i).astype(BF16)
        start(remote(hx.at[:, cols], hx_in.at[:, cols], h_s.at[i], h_r.at[i], mate))

    def own(i):
        acc[:, pl.ds(i * ROWS, ROWS)] = part(0, i)

    def gradients(i):
        cols = pl.ds(i * ROWS, ROWS)
        remote(hx.at[:, cols], hx_in.at[:, cols], h_s.at[i], h_r.at[i], mate).wait_recv()
        total = acc[:, cols] + hx_in[:, cols].astype(F32)
        gg[:, cols] = (total * factor[:, cols]).astype(BF16)
        gu[:, cols] = (total * act[:, cols]).astype(BF16)
        for n, (here, there) in enumerate(((gg, gg_hbm), (gu, gu_hbm))):
            out = pltpu.make_async_copy(
                here.at[:, cols], there.at[:, cols], out_sem.at[2 * i + n]
            )
            out.start()
            outs.append(out)

    def pump(events, lag=LAG):
        for _ in range(events):
            if state["event"] < NM:
                w_event(lag)
            if state["ready"] and state["todo"]:
                i = state["todo"].pop(0)
                mates(i, 0)
                state["own"].append(i)
            elif state["whole"] and state["own"]:
                i = state["own"].pop(0)
                own(i)
                if i > 1:
                    gradients(i - 2)

    def make_hidden(i, carry):
        rows = pl.ds(pl.multiple_of(i * 16, 16), 16)
        g = gate[rows, :].astype(F32)
        u = up[rows, :].astype(F32)
        sigma = jax.nn.sigmoid(g)
        activated = g * sigma
        act[rows, :] = activated
        factor[rows, :] = u * sigma * (1.0 + g * (1.0 - sigma))
        hidden[c, rows, :] = (activated * u).astype(BF16)
        return carry

    def hidden_now():
        loads[3].wait()
        loads[4].wait()
        lax.fori_loop(0, 16, make_hidden, 0)

    def to_second(ref, i):
        return remote(ref, ref, sib_s.at[i], sib_r.at[i], sibling)

    def low_rank_part():
        to_second(cot_own.at[0], 0).wait_recv()
        part = nt_dot(pbuf[...], cot_own[...].reshape(2 * ROWS, 512))
        part = part.reshape(NT, 64, 2 * ROWS)
        lr_full[...] = part
        lr_part[...] = part.astype(BF16)

    def low_rank_scatter():
        for k in range(1, NT):
            to = peer(k)
            start(remote(
                lr_part.at[to], lr_recv.at[k - 1], rs_s.at[k - 1], rs_r.at[k - 1],
                {"tensor": to},
            ))

    def low_rank_sum():
        total = lr_full[t]
        for k in range(1, NT):
            remote(
                lr_part.at[t], lr_recv.at[k - 1], rs_s.at[k - 1], rs_r.at[k - 1], pair
            ).wait_recv()
            total = total + lr_recv[k - 1].astype(F32)
        low_rank[t] = total.astype(BF16)

    def low_rank_gather():
        for k in range(1, NT):
            ref = low_rank.at[t]
            start(remote(
                ref, ref, ag_s.at[k - 1], ag_r.at[k - 1], {"tensor": peer(k)}
            ))

    def low_rank_wait():
        for k in range(1, NT):
            ref = low_rank.at[peer_back(k)]
            remote(
                ref, ref, ag_s.at[k - 1], ag_r.at[k - 1], {"tensor": peer_back(k)}
            ).wait_recv()

    def grad_tile(n, carry):
        at = lane(n * 256, 256)
        both = jnp.concatenate([hidden[0, :, at], hidden[1, :, at]], axis=0)
        part = jnp.dot(
            low_rank[...].reshape(512, 2 * ROWS), both, preferred_element_type=F32
        )
        pg[:, :, at] = part.reshape(NZ, 64, 256)
        return carry

    def own_part(zz, h):
        return pg[lax.rem(zz + NZ, NZ), :, pl.ds(h * HALF, HALF)]

    def turn(way, h):
        return (1 - 2 * way) * (1 - 2 * h)

    def ring(way, step, h):
        i = way * 4 + step
        return remote(
            ring_send.at[h, i], ring_recv.at[h, i], z_s.at[h, i], z_r.at[h, i],
            zdev(turn(way, h)),
        )

    def ring_step(step, h):
        for way in (0, 1):
            if step < 4 - way:
                i = way * 4 + step
                value = own_part(z + turn(way, h) * (4 - way - step), h)
                if step > 0:
                    ring(way, step - 1, h).wait_recv()
                    value = value + ring_recv[h, i - 1].astype(F32)
                ring_send[h, i] = value.astype(BF16)
        for way in (0, 1):
            if step < 4 - way:
                start(ring(way, step, h))

    def replica_send(h):
        ring(1, 2, h).wait_recv()
        value = own_part(z, h) + ring_recv[h, 6].astype(F32)
        ring(0, 3, h).wait_recv()
        value = value + ring_recv[h, 3].astype(F32)
        rep[h] = value.astype(BF16)
        there = rep_hbm.at[r, :, pl.ds(h * HALF, HALF)]
        for k in range(NR):
            for core in (0, 1):
                mine = rep.at[h, pl.ds(core * 32, 32), :]
                if (k, core) == (0, 1):
                    out = pltpu.make_async_copy(mine, there, out_sem.at[2 * STREAMS + h])
                    out.start()
                    outs.append(out)
                else:
                    start(remote(
                        mine, there, r_s.at[core, h, k], r_r.at[core, h, k],
                        {"replica": lax.rem(r + k, NR), "fsdp": z * 2 + core},
                    ))

    def finish(core):
        for i in range(STREAMS - 2, STREAMS):
            gradients(i)
        for h in (0, 1):
            for k in range(core, NR):
                back = lax.rem(r - k + NR, NR)
                remote(
                    rep.at[h, pl.ds(0, 32), :], rep_hbm.at[back, :, pl.ds(h * HALF, HALF)],
                    r_s.at[core, h, k], r_r.at[core, h, k], sibling,
                ).wait_recv()
        for copy in sent:
            copy.wait_send()
        for copy in outs:
            copy.wait()
        sent.clear()
        outs.clear()

    @pl.when(c == 0)
    def _():
        loads[0].wait()
        start(p_pass(z * 64, 32, sibling, 0, 0))
        c_begin()
        start(to_second(cot_own.at[0], 0))
        loads[1].wait()
        for i in range(STREAMS):
            start(w_own(i, 0))
        hidden_now()
        start(to_second(hidden.at[0], 1))
        w_push(-1, LAG)
        c_mates()
        pump(1)
        c_pair_wait(1)
        c_whole(1 - yl, 1, 1)
        c_forward(yl, 1, 0)
        pump(3)
        c_forward(1 - yl, 1, 1)
        pump(3)
        c_last(yl, 1, 0)
        c_last(1 - yl, 1, 1)
        state["ready"] = True
        c_pair_wait(0)
        c_whole(1 - yl, 0, 1)
        c_forward(yl, 0, 0)
        pump(4)
        c_forward(1 - yl, 0, 1)
        pump(4)
        c_last(yl, 0, 0)
        c_last(1 - yl, 0, 1)
        state["whole"] = True
        pump(NM)
        assert not state["todo"] and not state["own"]
        finish(0)

    @pl.when(c == 1)
    def _():
        loads[1].wait()
        for i in range(STREAMS):
            start(w_own(i, 1))
        loads[0].wait()
        p_pass(z * 64, 32, sibling, 0, 0).wait_recv()
        p_relay(0)
        c_begin()
        p_relay(1)
        p_relay(2)
        c_mates()
        p_relay(3)
        p_relay(4)
        low_rank_part()
        low_rank_scatter()
        c_pair_wait(1)
        c_whole(1 - yl, 1, 1)
        hidden_now()
        c_forward(yl, 1, 0)
        low_rank_sum()
        low_rank_gather()
        c_forward(1 - yl, 1, 1)
        c_pair_wait(0)
        c_whole(1 - yl, 0, 1)
        c_forward(yl, 0, 0)
        low_rank_wait()
        to_second(hidden.at[0], 1).wait_recv()
        lax.fori_loop(0, FF // 256, grad_tile, 0)
        ring_step(0, 0)
        ring_step(0, 1)
        c_last(yl, 1, 0)
        c_last(1 - yl, 1, 1)
        c_forward(1 - yl, 0, 1)
        mates(0, 1)
        ring_step(1, 0)
        ring_step(1, 1)
        c_last(yl, 0, 0)
        c_last(1 - yl, 0, 1)
        own(0)
        ring_step(2, 0)
        ring_step(2, 1)
        mates(1, 1)
        ring_step(3, 0)
        ring_step(3, 1)
        mates(2, 1)
        replica_send(0)
        replica_send(1)
        own(1)
        for i in range(3, STREAMS):
            mates(i, 1)
            own(i - 1)
            gradients(i - 3)
        own(STREAMS - 1)
        gradients(STREAMS - 3)
        finish(1)


def tail(scale, gg_in, gu_in, parts_in, gg, gu, pg, gg_v, gu_v, parts_v, pg_v, sems):
    quarters = []
    for n, (here, buffer, there) in enumerate(((gg_in, gg_v, gg), (gu_in, gu_v, gu))):
        for q in range(4):
            rows = pl.ds(q * 64, 64)
            i = n * 4 + q
            quarters.append((
                pltpu.make_async_copy(here.at[rows], buffer.at[rows], sems.at[0, i]),
                pltpu.make_async_copy(buffer.at[rows], there.at[rows], sems.at[1, i]),
            ))
    parts = pltpu.make_async_copy(parts_in, parts_v, sems.at[0, 8])
    result = pltpu.make_async_copy(pg_v, pg, sems.at[1, 8])
    parts.start()
    for load, _ in quarters:
        load.start()
    parts.wait()
    total = parts_v[0].astype(F32)
    for k in range(1, NR):
        total = total + parts_v[k].astype(F32)
    pg_v[...] = total * scale
    result.start()
    for load, store in quarters:
        load.wait()
        store.start()
    for _, store in quarters:
        store.wait()
    result.wait()


def local(cotangent, gate_pre, up_pre, down_weight, projector):
    rows, width = cotangent.shape
    ff = gate_pre.shape[1]
    tokens = rows * lax.axis_size("replica") * lax.axis_size("fsdp")
    scale = 1.0 / math.sqrt(tokens)
    dma = pltpu.SemaphoreType.DMA
    hbm = pl.BlockSpec(memory_space=pl.ANY)
    grad_gate, grad_up, parts = pl.pallas_call(
        kernel,
        out_shape=(
            jax.ShapeDtypeStruct((rows, ff), BF16),
            jax.ShapeDtypeStruct((rows, ff), BF16),
            jax.ShapeDtypeStruct((NR, 32, ff), BF16),
        ),
        in_specs=[hbm] * 5,
        out_specs=(hbm,) * 3,
        scratch_shapes=[
            pltpu.VMEM((ff, 2048), BF16),
            pltpu.VMEM((2 * rows, 2048), BF16),
            pltpu.VMEM((2, rows, width), BF16),
            pltpu.VMEM((512, width), BF16),
            pltpu.VMEM((rows, ff), BF16),
            pltpu.VMEM((rows, ff), BF16),
            pltpu.VMEM((rows, ff), F32),
            pltpu.VMEM((rows, ff), F32),
            pltpu.VMEM((2, rows, ff), BF16),
            pltpu.VMEM((rows, ff), F32),
            pltpu.VMEM((rows, ff), BF16),
            pltpu.VMEM((rows, ff), BF16),
            pltpu.VMEM((rows, ff), BF16),
            pltpu.VMEM((rows, ff), BF16),
            pltpu.VMEM((NT, 64, 2 * rows), F32),
            pltpu.VMEM((NT, 64, 2 * rows), BF16),
            pltpu.VMEM((NT - 1, 64, 2 * rows), BF16),
            pltpu.VMEM((NT, 64, 2 * rows), BF16),
            pltpu.VMEM((NZ, 64, ff), F32),
            pltpu.VMEM((2, 7, 64, HALF), BF16),
            pltpu.VMEM((2, 7, 64, HALF), BF16),
            pltpu.VMEM((2, 64, HALF), BF16),
            dma((7,)), dma((2 * STREAMS + 2,)),
            dma((2, NM)), dma((2, NM)), dma((2, NM)), dma((2, NM)),
            dma((2, NZ)), dma((2, NZ)), dma((2,)), dma((2,)),
            dma((2, STREAMS)), dma((2, STREAMS)),
            dma((3, 2, 4)), dma((3, 2, 4)), dma((2,)), dma((2,)),
            dma((7,)), dma((7,)), dma((7,)), dma((7,)),
            dma((2, 7)), dma((2, 7)), dma((2, 2, NR)), dma((2, 2, NR)),
            dma((STREAMS,)), dma((STREAMS,)),
        ],
        compiler_params=pltpu.CompilerParams(
            collective_id=0, has_side_effects=True, vmem_limit_bytes=56000 * 1024
        ),
        name="mlp_backward",
    )(cotangent, gate_pre, up_pre, down_weight, projector.T)

    return pl.pallas_call(
        functools.partial(tail, scale),
        out_shape=(
            jax.ShapeDtypeStruct((rows, ff), BF16),
            jax.ShapeDtypeStruct((rows, ff), BF16),
            jax.ShapeDtypeStruct((32, ff), F32),
        ),
        in_specs=[hbm] * 3,
        out_specs=(hbm,) * 3,
        scratch_shapes=[
            pltpu.VMEM((rows, ff), BF16),
            pltpu.VMEM((rows, ff), BF16),
            pltpu.VMEM((NR, 32, ff), BF16),
            pltpu.VMEM((32, ff), F32),
            dma((2, 9)),
        ],
        name="outputs",
    )(grad_gate, grad_up, parts)


def solution(mesh):
    placed = (
        P(("replica", "fsdp"), "tensor"),
        P(("replica", "fsdp"), "tensor"),
        P(("replica", "fsdp"), "tensor"),
        P("tensor", "fsdp"),
        P("tensor", "fsdp"),
    )
    return jax.shard_map(
        local,
        mesh=mesh,
        in_specs=placed,
        out_specs=(
            P(("replica", "fsdp"), "tensor"),
            P(("replica", "fsdp"), "tensor"),
            P("fsdp", "tensor"),
        ),
        check_vma=False,
    )
```
